32 devices in a mesh: grp: 2 (over x), xy: 4 (over z), guide: 4 (over y, core).
Axes of the slice: x: 2, y: 2, z: 4, core: 2. Of those that a mesh axis runs over, the one named last changes fastest.
Arguments:
- fields: float32 [2, 128, 36864], P('grp', 'guide', 'xy'), may hold values from -6 to 6
- rod_coeffs: float32 [3, 128, 4096], P(None, 'guide', 'xy'), may hold values from 0.08 to 0.32
- rod_mask: int32 [128, 4096], P('guide', 'xy'), may hold values 0 or 1
- pair_counts: int32 [4, 4], replicated, may hold values from 0 to 32, as said below
- fluid_slots: int32 [4, 4, 32], P('xy'), may hold values from 0 to 2303, as said below
- rod_slots: int32 [4, 4, 32], P('xy'), may hold values from 0 to 1023, as said below
- rod_sides: int32 [4, 4, 32], P('xy'), may hold values from 0 to 3, as said below
Outputs:
- fields_out: float32 [2, 128, 36864], P('grp', 'guide', 'xy')
The draws below stay inside these ranges and needn't reach their ends.
Inputs may be any that keep to these rules, and one draw needn't show every extreme that they name: `pair_counts`: block [j, o] is empty where tile j + offset_o would lie past the last tile along y (o = 1, 3) or along x (o = 2, 3); block 0 of every owner holds 16 or more slots; one owner, drawn from the seed, has all its non-empty-able blocks full (32 slots). `fluid_slots`: A water column of tile t, numbered x * 48 + y, one cell out from the face of the rod in the same slot. `rod_slots`: A cell of owner j numbered rod * 16 * 16 + x * 16 + y that lies on the face of its rod named by rod_sides, also in slots past the count. `rod_sides`: 0, 1, 2, 3 name the faces x = 0, x = 15, y = 0, y = 15 of a rod, with outward normals -x, +x, -y, +y.
All inputs are finite; a program needn't handle non-finite values. No bound on the sum of `rod_mask` on one device may be relied on, other than what follows from the above.
Results may differ from the reference program's by a relative error of at most 0.00002.
Values sent between devices are 32-bit elements; how exact they have to be, the bound alone decides.
A program may use at most 64 MiB of HBM per device.

```python
import math
import jax
import jax.numpy as jnp
from jax import lax

RODS_DEV = 4
S_ROD = 16
CY = 48
SLOTS = 32
FOOT = 4
STEPS = 4
TILES_Y = 4
ROD_COLS = 1024
LEVEL_VALUES = 9216
CX = 48
TILES_X = 1
NX = 48
NY = 192
NZ = 128
N_XY = 4


def foot_offsets():
    return jnp.array([0, 1, TILES_Y, TILES_Y + 1], dtype=jnp.int32)


def draw_pair_counts(key, part):
    owners = jnp.arange(N_XY, dtype=jnp.int32)[:, None]
    foot_ids = jnp.arange(FOOT, dtype=jnp.int32)[None, :]
    along_y_ok = owners % TILES_Y < TILES_Y - 1
    along_x_ok = owners // TILES_Y < TILES_X - 1
    allowed = jnp.where(foot_ids == 0, True, jnp.where(foot_ids == 1, along_y_ok, jnp.where(foot_ids == 2, along_x_ok, along_y_ok & along_x_ok)))
    first_counts = jax.random.randint(jax.random.fold_in(key, 11), (N_XY, FOOT), SLOTS // 2, SLOTS + 1)
    other_counts = jax.random.randint(jax.random.fold_in(key, 12), (N_XY, FOOT), 1, SLOTS + 1)
    in_use = jax.random.randint(jax.random.fold_in(key, 13), (N_XY, FOOT), 0, 2) == 1
    counts = jnp.where(foot_ids == 0, first_counts, jnp.where(in_use, other_counts, 0))
    busy_y = jax.random.randint(jax.random.fold_in(key, 14), (), 0, TILES_Y - 1)
    busy_x = jax.random.randint(jax.random.fold_in(key, 15), (), 0, max(TILES_X - 1, 1))
    busiest = busy_x * TILES_Y + busy_y
    counts = jnp.where(owners == busiest, SLOTS, counts)
    return jnp.where(allowed, counts, 0).astype(jnp.int32)


def rod_entries(key):
    entry_key = jax.random.fold_in(key, 21)
    shape_all = (N_XY, FOOT, SLOTS)
    rod_number = jax.random.randint(jax.random.fold_in(entry_key, 1), shape_all, 0, RODS_DEV)
    along_face = jax.random.randint(jax.random.fold_in(entry_key, 2), shape_all, 0, S_ROD)
    face_side = jax.random.randint(jax.random.fold_in(entry_key, 3), shape_all, 0, 4)
    across_face = jnp.where(face_side % 2 == 1, S_ROD - 1, 0)
    cell_x = jnp.where(face_side < 2, across_face, along_face)
    cell_y = jnp.where(face_side < 2, along_face, across_face)
    anchor_x = jax.random.randint(jax.random.fold_in(entry_key, 4), (N_XY, FOOT, RODS_DEV), 0, CX)
    anchor_y = jax.random.randint(jax.random.fold_in(entry_key, 5), (N_XY, FOOT, RODS_DEV), 0, CY)
    base_x = jnp.take_along_axis(anchor_x, rod_number, axis=2)
    base_y = jnp.take_along_axis(anchor_y, rod_number, axis=2)
    step_x = jnp.where(face_side == 0, -1, jnp.where(face_side == 1, 1, 0))
    step_y = jnp.where(face_side == 2, -1, jnp.where(face_side == 3, 1, 0))
    water_x = (base_x + cell_x + step_x) % CX
    water_y = (base_y + cell_y + step_y) % CY
    return (rod_number * S_ROD * S_ROD + cell_x * S_ROD + cell_y, face_side, water_x * CY + water_y)


def draw_rod_slots(key, part):
    return rod_entries(key)[0].astype(jnp.int32)


def draw_rod_sides(key, part):
    return rod_entries(key)[1].astype(jnp.int32)


def draw_fluid_slots(key, part):
    water_cols = rod_entries(key)[2]
    tile_ids = jnp.arange(N_XY, dtype=jnp.int32)[:, None]
    sources = (tile_ids - foot_offsets()[None, :]) % N_XY
    foot_ids = jnp.arange(FOOT, dtype=jnp.int32)[None, :]
    return water_cols[sources, foot_ids].astype(jnp.int32)


def set_ends(drawn, rng, least, largest):
    shape = drawn.shape
    index_at = [jax.random.randint(jax.random.fold_in(rng, axis), (), 0, shape[axis]) for axis in range(len(shape))]
    drawn = drawn.at[tuple(index_at)].set(least)
    longest = shape.index(max(shape))
    index_at[longest] = (index_at[longest] + 1) % shape[longest]
    return drawn.at[tuple(index_at)].set(largest)


def steps_of(rng, extent, pieces, smallest, top_value):
    level, own = 1.0, jax.random.fold_in(rng, 6)
    for dim, blocks in pieces:
        steps = jnp.exp(jax.random.uniform(jax.random.fold_in(own, dim), (blocks,), jnp.float32, smallest / len(pieces), top_value / len(pieces)))
        level = level * jnp.repeat(steps, extent[dim] // blocks).reshape([-1 if axis == dim else 1 for axis in range(len(extent))])
    return level


def scatter_about(key, dims, spread, reach, shards=(), kind=jnp.bfloat16):
    entries = spread * jax.random.normal(key, dims, jnp.float32)
    if shards:
        entries = entries * steps_of(key, dims, shards, -0.22, 0.18)
    return jnp.clip(entries, -reach, reach).astype(kind)


def setup_inputs(seed: int = 0) -> dict:
    seeds = jax.random.split(jax.random.key(seed), 8)
    fields = scatter_about(seeds[0], (2, NZ, N_XY * LEVEL_VALUES), 1.0, 6.0, ((0, 2), (1, 4), (2, 4)), jnp.float32)
    rod_coeffs = jnp.clip(jnp.exp(math.log(0.32) - 1.3862944 * jax.random.uniform(seeds[1], (3, NZ, N_XY * ROD_COLS), jnp.float32) ** steps_of(seeds[1], (3, NZ, N_XY * ROD_COLS), ((1, 4), (2, 4)), -0.2, 0.2)), 0.08, 0.32)
    rod_mask = set_ends((jax.random.randint(seeds[2], (NZ, N_XY * ROD_COLS), 0, 2) < 1).astype(jnp.int32), jax.random.fold_in(seeds[2], 1), 0, 1)
    pair_counts = draw_pair_counts(jax.random.fold_in(seeds[7], 71), 0)
    fluid_slots = draw_fluid_slots(jax.random.fold_in(seeds[7], 71), 0)
    rod_slots = draw_rod_slots(jax.random.fold_in(seeds[7], 71), 0)
    rod_sides = draw_rod_sides(jax.random.fold_in(seeds[7], 71), 0)
    return dict(fields=fields, rod_coeffs=rod_coeffs, rod_mask=rod_mask, pair_counts=pair_counts, fluid_slots=fluid_slots, rod_slots=rod_slots, rod_sides=rod_sides)


FLUID_A = 0.55
FLUID_B = 0.5
SOFT_SHARE = 0.35


def fore_diff(values, along):
    length = values.shape[along]
    later_cells = jnp.concatenate([lax.slice_in_dim(values, 1, length, axis=along), jnp.zeros_like(lax.slice_in_dim(values, 0, 1, axis=along))], axis=along)
    return later_cells - values


def back_diff(values, along):
    length = values.shape[along]
    before = jnp.concatenate([jnp.zeros_like(lax.slice_in_dim(values, 0, 1, axis=along)), lax.slice_in_dim(values, 0, length - 1, axis=along)], axis=along)
    return values - before


def fore_wrap(values):
    return jnp.roll(values, -1, axis=0) - values


def back_wrap(values):
    return values - jnp.roll(values, 1, axis=0)


def reference(fields, rod_coeffs, rod_mask, pair_counts, fluid_slots, rod_slots, rod_sides):
    rod_cols = RODS_DEV * S_ROD * S_ROD
    all_rods = N_XY * RODS_DEV
    all_cols = N_XY * rod_cols
    rod_grid = (NZ, all_rods, S_ROD, S_ROD)
    solid_part = fields[0].reshape(NZ, N_XY, 9, rod_cols).transpose(2, 0, 1, 3).reshape((9,) + rod_grid)
    fluid_part = fields[1].reshape(NZ, TILES_X, TILES_Y, 4, CX, CY).transpose(3, 0, 1, 4, 2, 5).reshape(4, NZ, NX, NY)
    softness = jnp.where(rod_mask == 1, 1.0, SOFT_SHARE).astype(jnp.float32).reshape(rod_grid)
    coeffs = rod_coeffs.reshape((3,) + rod_grid)
    lame_first = coeffs[0] * softness
    shear_mod = coeffs[1] * softness
    buoyancy = coeffs[2]
    offsets = jnp.array([0, 1, TILES_Y, TILES_Y + 1], dtype=jnp.int32)
    owner_ids = jnp.arange(N_XY, dtype=jnp.int32)[:, None, None]
    foot_ids = jnp.arange(FOOT, dtype=jnp.int32)[None, :]
    slot_ids = jnp.arange(SLOTS, dtype=jnp.int32)[None, None, :]
    tile_of = ((owner_ids[:, :, 0] + offsets[None, :]) % N_XY).astype(jnp.int32)
    water_slots = fluid_slots[tile_of, foot_ids]
    valid_rows = (slot_ids < pair_counts[:, :, None]).astype(jnp.float32).reshape(-1)
    grid_x = (tile_of[:, :, None] // TILES_Y) * CX + water_slots // CY
    grid_y = (tile_of[:, :, None] % TILES_Y) * CY + water_slots % CY
    fluid_col = (grid_x * NY + grid_y).reshape(-1).astype(jnp.int32)
    facing = (2 * (rod_sides % 2) - 1).astype(jnp.float32).reshape(-1)
    target = ((rod_sides // 2) * all_cols + owner_ids * rod_cols + rod_slots).reshape(-1).astype(jnp.int32)
    speed_x, speed_y, speed_z, stress_xx, stress_yy, stress_zz, stress_xy, stress_xz, stress_yz = solid_part
    pressure, flow_x, flow_y, flow_z = fluid_part
    for repeat in range(STEPS):
        sampled = pressure.reshape(NZ, NX * NY)[:, fluid_col]
        traction = jnp.zeros((NZ, 2 * all_cols), jnp.float32).at[:, target].add(sampled * (-facing * valid_rows))
        traction_x = traction[:, :all_cols].reshape(rod_grid)
        traction_y = traction[:, all_cols:].reshape(rod_grid)
        speed_x = speed_x + buoyancy * (fore_diff(stress_xx, 2) + back_diff(stress_xy, 3) + back_wrap(stress_xz) + traction_x)
        speed_y = speed_y + buoyancy * (back_diff(stress_xy, 2) + fore_diff(stress_yy, 3) + back_wrap(stress_yz) + traction_y)
        speed_z = speed_z + buoyancy * (back_diff(stress_xz, 2) + back_diff(stress_yz, 3) + fore_wrap(stress_zz))
        flow_x = flow_x - FLUID_B * fore_diff(pressure, 1)
        flow_y = flow_y - FLUID_B * fore_diff(pressure, 2)
        flow_z = flow_z - FLUID_B * fore_wrap(pressure)
        normal = jnp.concatenate([speed_x.reshape(NZ, all_cols), speed_y.reshape(NZ, all_cols)], axis=1)[:, target]
        inflow = jnp.zeros((NZ, NX * NY), jnp.float32).at[:, fluid_col].add(normal * (facing * valid_rows)).reshape(NZ, NX, NY)
        pressure = pressure + FLUID_A * (inflow - (back_diff(flow_x, 1) + back_diff(flow_y, 2) + back_wrap(flow_z)))
        spread_x = back_diff(speed_x, 2)
        spread_y = back_diff(speed_y, 3)
        spread_z = back_wrap(speed_z)
        volume = spread_x + spread_y + spread_z
        stress_xx = stress_xx + lame_first * volume + 2.0 * shear_mod * spread_x
        stress_yy = stress_yy + lame_first * volume + 2.0 * shear_mod * spread_y
        stress_zz = stress_zz + lame_first * volume + 2.0 * shear_mod * spread_z
        stress_xy = stress_xy + shear_mod * (fore_diff(speed_x, 3) + fore_diff(speed_y, 2))
        stress_xz = stress_xz + shear_mod * (fore_wrap(speed_x) + fore_diff(speed_z, 2))
        stress_yz = stress_yz + shear_mod * (fore_wrap(speed_y) + fore_diff(speed_z, 3))
    solid_end = jnp.stack([speed_x, speed_y, speed_z, stress_xx, stress_yy, stress_zz, stress_xy, stress_xz, stress_yz])
    solid_end = solid_end.reshape(9, NZ, N_XY, rod_cols).transpose(1, 2, 0, 3).reshape(NZ, N_XY * 9 * rod_cols)
    fluid_end = jnp.stack([pressure, flow_x, flow_y, flow_z])
    fluid_end = fluid_end.reshape(4, NZ, TILES_X, CX, TILES_Y, CY).transpose(1, 2, 4, 0, 3, 5).reshape(NZ, N_XY * 9 * rod_cols)
    return jnp.stack([solid_end, fluid_end])
```

```python
import functools

import jax
import jax.numpy as jnp
from jax import lax
from jax.experimental import pallas as pl
from jax.experimental.pallas import tpu as pltpu
from jax.sharding import PartitionSpec as P

S_ROD = 16
CY = 48
STEPS = 4
TILES_Y = 4

FLUID_A = 0.55
FLUID_B = 0.5
SOFT_SHARE = 0.35

LANES = 128
HALF = 64
CHUNK = 256
MESH = pl.DeviceIdType.MESH
F32 = jnp.float32
BF16 = jnp.bfloat16


def iota(shape, dim):
    return lax.broadcasted_iota(jnp.int32, shape, dim)


def split3(values):
    hi = values.astype(BF16)
    rest = values - hi.astype(F32)
    mid = rest.astype(BF16)
    low = (rest - mid.astype(F32)).astype(BF16)
    return jnp.concatenate([hi, mid, low], axis=0)


def join3(values):
    n = values.shape[0] // 3
    return values[:n] + values[n : 2 * n] + values[2 * n :]


def dot(a, b):
    return jnp.dot(a, b, preferred_element_type=F32)


def one_hot(cond):
    return jnp.where(cond, 1.0, 0.0).astype(BF16)


def kernel(
    n_xy,
    n_guide,
    f_ref,
    c_ref,
    m_ref,
    row_ref,
    col_ref,
    o_ref,
    g_ref,
    s_ref,
    y_ref,
    mm_ref,
    lame_ref,
    shear_ref,
    be_ref,
    ebase_ref,
    send_i,
    recv_i,
    send_y,
    recv_yu,
    recv_yd,
    send_rim,
    recv_rim,
    send_x,
    recv_x,
    send_sem,
    recv_sem,
):
    levels, width = o_ref.shape
    rc = width // 9
    tc = width // 4
    rows = tc // CY
    tiles_x = n_xy // TILES_Y
    grp = lax.axis_index("grp")
    xy = lax.axis_index("xy")
    guide = lax.axis_index("guide")
    col_y = lax.rem(xy, TILES_Y)
    col_x = xy // TILES_Y
    feet = [(0, 0), (0, 1)] + ([(1, 0), (1, 1)] if tiles_x > 1 else [])
    nf = len(feet)
    up_g = lax.rem(guide + 1, n_guide)
    down_g = lax.rem(guide + n_guide - 1, n_guide)
    YU, YD, RIM, XA, XB = nf, nf + 1, nf + 2, nf + 6, nf + 7

    def foot_has(o, solid):
        dx, dy = feet[o]
        if solid:
            return jnp.logical_and(col_y + dy < TILES_Y, col_x + dx < tiles_x)
        return jnp.logical_and(col_y >= dy, col_x >= dx)

    def foot_xy(o, solid):
        dx, dy = feet[o]
        off = dx * TILES_Y + dy
        return lax.rem(xy + off, n_xy) if solid else lax.rem(xy + n_xy - off, n_xy)

    def copy(src, dst, ch, s, device):
        return pltpu.make_async_remote_copy(
            src_ref=src,
            dst_ref=dst,
            send_sem=send_sem.at[ch, s],
            recv_sem=recv_sem.at[ch, s],
            device_id=device,
            device_id_type=MESH,
        )

    def c_foot(o, s, solid):
        return copy(
            send_i.at[s],
            recv_i.at[s, o],
            o,
            s,
            {"grp": 1 - grp, "xy": foot_xy(o, solid)},
        )

    def c_up(s):
        return copy(send_y.at[s], recv_yu.at[s], YU, s, {"xy": lax.rem(xy + n_xy - 1, n_xy)})

    def c_down(s):
        return copy(send_y.at[s], recv_yd.at[s], YD, s, {"xy": lax.rem(xy + 1, n_xy)})

    def c_rim(kind, s, size):
        cols = pl.ds(0, size)
        return copy(
            send_rim.at[kind, s, :, cols],
            recv_rim.at[kind, s, :, cols],
            RIM + kind,
            s,
            {"guide": down_g if kind % 2 else up_g},
        )

    def c_x(which, s):
        off = n_xy - TILES_Y if which == 0 else TILES_Y
        return copy(
            send_x.at[which, s],
            recv_x.at[which, s],
            XA + which,
            s,
            {"xy": lax.rem(xy + off, n_xy)},
        )

    has_next_y = col_y < TILES_Y - 1
    has_prev_y = col_y > 0
    has_next_x = col_x < tiles_x - 1
    has_prev_x = col_x > 0

    barrier = pltpu.get_barrier_semaphore()

    def greet(device):
        pl.semaphore_signal(barrier, inc=1, device_id=device, device_id_type=MESH)

    greet({"guide": up_g})
    greet({"guide": down_g})
    for solid in (True, False):
        for o in range(nf):
            mine = (grp == 0) if solid else (grp != 0)

            @pl.when(jnp.logical_and(mine, foot_has(o, solid)))
            def _():
                greet({"grp": 1 - grp, "xy": foot_xy(o, solid)})

    sides = [(has_next_y, 1), (has_prev_y, n_xy - 1)]
    if tiles_x > 1:
        sides += [(has_next_x, TILES_Y), (has_prev_x, n_xy - TILES_Y)]
    for has, off in sides:

        @pl.when(jnp.logical_and(grp != 0, has))
        def _():
            greet({"xy": lax.rem(xy + off, n_xy)})

    def as_int(cond):
        return jnp.where(cond, 1, 0)

    solid_n = sum(as_int(foot_has(o, True)) for o in range(nf))
    fluid_n = sum(as_int(foot_has(o, False)) for o in range(nf)) + sum(as_int(h) for h, _ in sides)
    expect = 2 + jnp.where(grp == 0, solid_n, fluid_n)

    row_idx = row_ref[0:1, :]
    facing = row_ref[1:2, :].astype(F32)
    lane = iota((levels, LANES), 1)
    level8 = iota((8, 1), 0)
    slots = LANES // 4

    def comp(ref, member, size, r0):
        return ref[r0 : r0 + 8, member * size : (member + 1) * size]

    def lower(member, size, r0, rim):
        if r0 == 0:
            block = comp(o_ref, member, size, 0)
            return jnp.where(level8 == 0, rim, pltpu.roll(block, 1, 0))
        return o_ref[r0 - 1 : r0 + 7, member * size : (member + 1) * size]

    def upper(member, size, r0, rim):
        if r0 == levels - 8:
            block = comp(o_ref, member, size, r0)
            return jnp.where(level8 == 7, rim, pltpu.roll(block, 7, 0))
        return o_ref[r0 + 1 : r0 + 9, member * size : (member + 1) * size]

    def gather(start, size, lanes):
        acc = None
        for c in range(0, size, CHUNK):
            part = dot(
                split3(o_ref[:, start + c : start + c + CHUNK]),
                g_ref[c : c + CHUNK, lanes[0] : lanes[1]],
            )
            acc = part if acc is None else acc + part
        return join3(acc)

    def incoming(s):
        arrived = recv_i[s, 0]
        for o in range(1, nf):
            arrived = jnp.where(lane >= o * slots, recv_i[s, o], arrived)
        return jnp.where(lane < nf * slots, arrived, 0.0)

    def each_foot(solid, act):
        for o in range(nf):

            @pl.when(foot_has(o, solid))
            def _():
                act(o)

    def no_feet(solid):
        for o in range(1, nf):

            @pl.when(jnp.logical_not(foot_has(o, solid)))
            def _():
                recv_i[:, o] = jnp.zeros((STEPS, levels, LANES), F32)

    @pl.when(grp == 0)
    def _():
        o_ref[...] = f_ref[...]
        no_feet(True)

        def put_a(s):
            top = levels - 1
            send_rim[0, s, :, 0 : 2 * rc] = o_ref[top : top + 1, 7 * rc : 9 * rc]
            send_rim[1, s, :, 0:rc] = o_ref[0:1, 5 * rc : 6 * rc]
            c_rim(0, s, 2 * rc).start()
            c_rim(1, s, rc).start()

        pl.semaphore_wait(barrier, expect)
        put_a(0)
        for c in range(0, 2 * rc, CHUNK):
            g_ref[c : c + CHUNK, 0:LANES] = one_hot(iota((CHUNK, LANES), 0) + c == row_idx)
            s_ref[0:LANES, c : c + CHUNK] = one_hot(iota((LANES, CHUNK), 1) + c == col_ref[...])
        mm_ref[0:LANES, 0:LANES] = one_hot(col_ref[...] == row_idx)
        for r0 in range(0, levels, 8):
            soft = jnp.where(m_ref[r0 : r0 + 8, :] == 1, 1.0, SOFT_SHARE).astype(F32)
            lame_ref[r0 : r0 + 8, :] = c_ref[0, r0 : r0 + 8, :] * soft
            shear_ref[r0 : r0 + 8, :] = c_ref[1, r0 : r0 + 8, :] * soft
        acc = None
        for c in range(0, 2 * rc, CHUNK):
            part = dot(
                split3(c_ref[2, :, c % rc : c % rc + CHUNK]), g_ref[c : c + CHUNK, 0:LANES]
            )
            acc = part if acc is None else acc + part
        be_ref[...] = join3(acc)

        place = iota((1, rc), 1)
        in_x = place // S_ROD % S_ROD
        in_y = place % S_ROD

        def fore_x(v):
            return jnp.where(in_x < S_ROD - 1, pltpu.roll(v, rc - S_ROD, 1), 0.0) - v

        def back_x(v):
            return v - jnp.where(in_x > 0, pltpu.roll(v, S_ROD, 1), 0.0)

        def fore_y(v):
            return jnp.where(in_y < S_ROD - 1, pltpu.roll(v, rc - 1, 1), 0.0) - v

        def back_y(v):
            return v - jnp.where(in_y > 0, pltpu.roll(v, 1, 1), 0.0)

        def store(member, r0, v):
            o_ref[r0 : r0 + 8, member * rc : (member + 1) * rc] = v

        def step(s, carry):
            c_rim(0, s, 2 * rc).wait_recv()
            c_rim(1, s, rc).wait_recv()
            for r0 in range(0, levels, 8):
                buo = c_ref[2, r0 : r0 + 8, :]
                xy_ = comp(o_ref, 6, rc, r0)
                xz = comp(o_ref, 7, rc, r0)
                yz = comp(o_ref, 8, rc, r0)
                xz_lo = lower(7, rc, r0, recv_rim[0, s, :, 0:rc])
                yz_lo = lower(8, rc, r0, recv_rim[0, s, :, rc : 2 * rc])
                store(
                    0,
                    r0,
                    comp(o_ref, 0, rc, r0)
                    + buo * (fore_x(comp(o_ref, 3, rc, r0)) + back_y(xy_) + (xz - xz_lo)),
                )
                store(
                    1,
                    r0,
                    comp(o_ref, 1, rc, r0)
                    + buo * (back_x(xy_) + fore_y(comp(o_ref, 4, rc, r0)) + (yz - yz_lo)),
                )
                zz = comp(o_ref, 5, rc, r0)
                zz_up = upper(5, rc, r0, recv_rim[1, s, :, 0:rc])
                store(
                    2,
                    r0,
                    comp(o_ref, 2, rc, r0) + buo * (back_x(xz) + back_y(yz) + (zz_up - zz)),
                )
            send_rim[2, s, :, 0:rc] = o_ref[levels - 1 : levels, 2 * rc : 3 * rc]
            c_rim(2, s, rc).start()
            base = gather(0, 2 * rc, (0, LANES))
            each_foot(True, lambda o: c_foot(o, s, True).wait_recv())
            lhs = split3(incoming(s) * (-facing))
            normal = base + be_ref[...] * join3(dot(lhs, mm_ref[0:LANES, 0:LANES]))
            send_i[s] = normal * facing
            each_foot(True, lambda o: c_foot(o, s, True).start())
            for c in range(0, 2 * rc, CHUNK):
                push = join3(dot(lhs, s_ref[0:LANES, c : c + CHUNK]))
                o_ref[:, c : c + CHUNK] += c_ref[2, :, c % rc : c % rc + CHUNK] * push
            send_rim[3, s, :, 0 : 2 * rc] = o_ref[0:1, 0 : 2 * rc]
            c_rim(3, s, 2 * rc).start()
            c_rim(2, s, rc).wait_recv()
            c_rim(3, s, 2 * rc).wait_recv()
            for r0 in range(0, levels, 8):
                sx = comp(o_ref, 0, rc, r0)
                sy = comp(o_ref, 1, rc, r0)
                sz = comp(o_ref, 2, rc, r0)
                lame = lame_ref[r0 : r0 + 8, :]
                shear = shear_ref[r0 : r0 + 8, :]
                spread_x = back_x(sx)
                spread_y = back_y(sy)
                spread_z = sz - lower(2, rc, r0, recv_rim[2, s, :, 0:rc])
                bulk = lame * (spread_x + spread_y + spread_z)
                twice = 2.0 * shear
                store(3, r0, comp(o_ref, 3, rc, r0) + bulk + twice * spread_x)
                store(4, r0, comp(o_ref, 4, rc, r0) + bulk + twice * spread_y)
                store(5, r0, comp(o_ref, 5, rc, r0) + bulk + twice * spread_z)
                store(6, r0, comp(o_ref, 6, rc, r0) + shear * (fore_y(sx) + fore_x(sy)))
                sx_up = upper(0, rc, r0, recv_rim[3, s, :, 0:rc])
                sy_up = upper(1, rc, r0, recv_rim[3, s, :, rc : 2 * rc])
                store(7, r0, comp(o_ref, 7, rc, r0) + shear * (sx_up - sx + fore_x(sz)))
                store(8, r0, comp(o_ref, 8, rc, r0) + shear * (sy_up - sy + fore_y(sz)))

            @pl.when(s < STEPS - 1)
            def _():
                put_a(s + 1)

            return carry

        lax.fori_loop(0, STEPS, step, 0)

        def drain(s, carry):
            for kind, size in ((0, 2 * rc), (1, rc), (2, rc), (3, 2 * rc)):
                c_rim(kind, s, size).wait_send()
            each_foot(True, lambda o: c_foot(o, s, True).wait_send())
            return carry

        lax.fori_loop(0, STEPS, drain, 0)

    @pl.when(grp != 0)
    def _():
        o_ref[...] = f_ref[...]
        no_feet(False)

        @pl.when(jnp.logical_not(has_next_y))
        def _():
            recv_yu[...] = jnp.zeros_like(recv_yu)

        @pl.when(jnp.logical_not(has_prev_y))
        def _():
            recv_yd[...] = jnp.zeros_like(recv_yd)

        if tiles_x > 1:

            @pl.when(jnp.logical_not(has_next_x))
            def _():
                recv_x[0] = jnp.zeros((STEPS, levels, LANES), F32)

            @pl.when(jnp.logical_not(has_prev_x))
            def _():
                recv_x[1] = jnp.zeros((STEPS, levels, LANES), F32)

        pl.semaphore_wait(barrier, expect)
        edge = iota((1, LANES), 1)
        edge_cols = jnp.where(
            edge < rows,
            edge * CY,
            jnp.where(
                jnp.logical_and(edge >= HALF, edge < HALF + rows),
                (edge - HALF) * CY + CY - 1,
                -2,
            ),
        )
        spot = iota((LANES, 1), 0)
        first_spots = jnp.where(spot < rows, spot * CY, -1)
        last_spots = jnp.where(spot < rows, spot * CY + CY - 1, -1)

        def put_rim(s):
            send_rim[1, s, :, 0:tc] = o_ref[0:1, 0:tc]
            c_rim(1, s, tc).start()
            if tiles_x > 1:
                send_x[0, s] = o_ref[:, 0:LANES]

                @pl.when(has_prev_x)
                def _():
                    c_x(0, s).start()

        def put_samples(s, samples):
            send_i[s] = samples[:, :LANES]
            send_y[s] = samples[:, LANES:]
            each_foot(False, lambda o: c_foot(o, s, False).start())

            @pl.when(has_prev_y)
            def _():
                c_up(s).start()

            @pl.when(has_next_y)
            def _():
                c_down(s).start()

        put_rim(0)
        for c in range(0, tc, CHUNK):
            g_ref[c : c + CHUNK, 0:LANES] = one_hot(iota((CHUNK, LANES), 0) + c == row_idx)
            g_ref[c : c + CHUNK, LANES:] = one_hot(iota((CHUNK, LANES), 0) + c == edge_cols)
        put_samples(0, gather(0, tc, (0, 2 * LANES)))
        send_y[STEPS] = gather(2 * tc, tc, (LANES, 2 * LANES))

        @pl.when(has_next_y)
        def _():
            c_down(STEPS).start()

        for c in range(0, tc, CHUNK):
            at = iota((LANES, CHUNK), 1) + c
            s_ref[0:LANES, c : c + CHUNK] = one_hot(at == col_ref[...])
            s_ref[LANES:, c : c + CHUNK] = one_hot(at == first_spots)
            y_ref[:, c : c + CHUNK] = one_hot(at == last_spots)
        mm_ref[0:LANES, 0:LANES] = one_hot(col_ref[...] == row_idx)
        mm_ref[0:LANES, LANES:] = one_hot(col_ref[...] == edge_cols)
        mm_ref[LANES:, 0:LANES] = one_hot(first_spots == row_idx)
        mm_ref[LANES:, LANES:] = one_hot(first_spots == edge_cols)

        @pl.when(has_prev_y)
        def _():
            c_down(STEPS).wait_recv()

        be_ref[...] = jnp.where(lane < rows, pltpu.roll(recv_yd[STEPS], HALF, 1), 0.0)

        place = iota((1, tc), 1)
        in_y = place % CY

        def store(member, r0, v):
            o_ref[r0 : r0 + 8, member * tc : (member + 1) * tc] = v

        def step(s, carry):
            c_rim(1, s, tc).wait_recv()
            if tiles_x > 1:

                @pl.when(has_next_x)
                def _():
                    c_x(0, s).wait_recv()

            for r0 in range(0, levels, 8):
                p = comp(o_ref, 0, tc, r0)
                next_x = jnp.where(place < tc - CY, pltpu.roll(p, tc - CY, 1), 0.0)
                store(1, r0, comp(o_ref, 1, tc, r0) - FLUID_B * (next_x - p))
                next_y = jnp.where(in_y < CY - 1, pltpu.roll(p, tc - 1, 1), 0.0)
                store(2, r0, comp(o_ref, 2, tc, r0) - FLUID_B * (next_y - p))
                next_z = upper(0, tc, r0, recv_rim[1, s, :, 0:tc])
                store(3, r0, comp(o_ref, 3, tc, r0) - FLUID_B * (next_z - p))
            send_rim[2, s, :, 0:tc] = o_ref[levels - 1 : levels, 3 * tc : 4 * tc]
            c_rim(2, s, tc).start()
            if tiles_x > 1:
                ahead = pltpu.roll(recv_x[0, s], LANES - CY, 1)
                tail = slice(2 * tc - LANES, 2 * tc)
                o_ref[:, tail] -= jnp.where(lane >= LANES - CY, FLUID_B * ahead, 0.0)
                send_x[1, s] = o_ref[:, tail]

                @pl.when(has_next_x)
                def _():
                    c_x(1, s).start()

            @pl.when(has_next_y)
            def _():
                c_up(s).wait_recv()

            @pl.when(has_prev_y)
            def _():
                c_down(s).wait_recv()

            lhs = split3(recv_yu[s])
            for c in range(0, tc, CHUNK):
                o_ref[:, 2 * tc + c : 2 * tc + c + CHUNK] -= FLUID_B * join3(
                    dot(lhs, y_ref[:, c : c + CHUNK])
                )
            behind = be_ref[...] - FLUID_B * (send_y[s] - pltpu.roll(recv_yd[s], HALF, 1))
            behind = jnp.where(jnp.logical_and(lane < rows, has_prev_y), behind, 0.0)
            be_ref[...] = behind

            c_rim(2, s, tc).wait_recv()
            for r0 in range(0, levels, 8):
                fx = comp(o_ref, 1, tc, r0)
                fy = comp(o_ref, 2, tc, r0)
                fz = comp(o_ref, 3, tc, r0)
                prev_x = jnp.where(place >= CY, pltpu.roll(fx, CY, 1), 0.0)
                prev_y = jnp.where(in_y > 0, pltpu.roll(fy, 1, 1), 0.0)
                prev_z = lower(3, tc, r0, recv_rim[2, s, :, 0:tc])
                store(
                    0,
                    r0,
                    comp(o_ref, 0, tc, r0)
                    - FLUID_A * ((fx - prev_x) + (fy - prev_y) + (fz - prev_z)),
                )
            if tiles_x > 1:

                @pl.when(has_prev_x)
                def _():
                    c_x(1, s).wait_recv()

                before = pltpu.roll(recv_x[1, s], CY, 1)
                o_ref[:, 0:LANES] += jnp.where(lane < CY, FLUID_A * before, 0.0)

            @pl.when(s < STEPS - 1)
            def _():
                ebase_ref[...] = gather(0, tc, (0, 2 * LANES))

            each_foot(False, lambda o: c_foot(o, s, False).wait_recv())
            lhs = split3(jnp.concatenate([incoming(s), behind], axis=1))

            @pl.when(s < STEPS - 1)
            def _():
                put_samples(
                    s + 1, ebase_ref[...] + FLUID_A * join3(dot(lhs, mm_ref[...]))
                )

            for c in range(0, tc, CHUNK):
                o_ref[:, c : c + CHUNK] += FLUID_A * join3(dot(lhs, s_ref[:, c : c + CHUNK]))

            @pl.when(s < STEPS - 1)
            def _():
                put_rim(s + 1)

            return carry

        lax.fori_loop(0, STEPS, step, 0)

        def drain(s, carry):
            c_rim(1, s, tc).wait_send()
            c_rim(2, s, tc).wait_send()
            each_foot(False, lambda o: c_foot(o, s, False).wait_send())

            @pl.when(has_prev_y)
            def _():
                c_up(s).wait_send()

            @pl.when(has_next_y)
            def _():
                c_down(s).wait_send()

            if tiles_x > 1:

                @pl.when(has_prev_x)
                def _():
                    c_x(0, s).wait_send()

                @pl.when(has_next_x)
                def _():
                    c_x(1, s).wait_send()

            return carry

        lax.fori_loop(0, STEPS, drain, 0)

        @pl.when(has_next_y)
        def _():
            c_down(STEPS).wait_send()


def local(n_xy, n_guide, fields, rod_coeffs, rod_mask, pair_counts, fluid_slots, rod_slots, rod_sides):
    levels, width = fields.shape[1:]
    rc, tc = width // 9, width // 4
    tile = lax.axis_index("xy")
    is_solid = lax.axis_index("grp") == 0
    slots = fluid_slots.shape[2]
    offsets = jnp.array([0, 1, TILES_Y, TILES_Y + 1], dtype=jnp.int32)
    owner_ids = jnp.arange(n_xy, dtype=jnp.int32)[:, None]
    owners = jnp.where(is_solid, tile, (tile - offsets) % n_xy)
    counts = jnp.sum(jnp.where(owner_ids == owners[None, :], pair_counts, 0), axis=0)
    valid = (jnp.arange(slots, dtype=jnp.int32)[None, :] < counts[:, None]).reshape(-1)
    sides = rod_sides[0].reshape(-1)
    cols = jnp.where(
        is_solid, sides // 2 * rc + rod_slots[0].reshape(-1), fluid_slots[0].reshape(-1)
    )
    facing = 2 * (sides % 2) - 1
    row = jnp.stack([cols, facing])
    col = jnp.where(valid, cols, -1).reshape(-1, 1)
    n_feet = 4 if n_xy > TILES_Y else 2
    n_x = 2 if n_xy > TILES_Y else 1
    x_steps = STEPS if n_xy > TILES_Y else 1
    rim = max(2 * rc, tc)
    vmem = pl.BlockSpec(memory_space=pltpu.VMEM)
    out = pl.pallas_call(
        functools.partial(kernel, n_xy, n_guide),
        out_shape=jax.ShapeDtypeStruct((levels, width), F32),
        in_specs=[vmem] * 5,
        out_specs=vmem,
        scratch_shapes=[
            pltpu.VMEM((tc, 2 * LANES), BF16),
            pltpu.VMEM((2 * LANES, tc), BF16),
            pltpu.VMEM((LANES, tc), BF16),
            pltpu.VMEM((2 * LANES, 2 * LANES), BF16),
            pltpu.VMEM((levels, rc), F32),
            pltpu.VMEM((levels, rc), F32),
            pltpu.VMEM((levels, LANES), F32),
            pltpu.VMEM((levels, 2 * LANES), F32),
            pltpu.VMEM((STEPS, levels, LANES), F32),
            pltpu.VMEM((STEPS, n_feet, levels, LANES), F32),
            pltpu.VMEM((STEPS + 1, levels, LANES), F32),
            pltpu.VMEM((STEPS + 1, levels, LANES), F32),
            pltpu.VMEM((STEPS + 1, levels, LANES), F32),
            pltpu.VMEM((4, STEPS, 1, rim), F32),
            pltpu.VMEM((4, STEPS, 1, rim), F32),
            pltpu.VMEM((n_x, x_steps, levels, LANES), F32),
            pltpu.VMEM((n_x, x_steps, levels, LANES), F32),
            pltpu.SemaphoreType.DMA((n_feet + 8, STEPS + 1)),
            pltpu.SemaphoreType.DMA((n_feet + 8, STEPS + 1)),
        ],
        compiler_params=pltpu.CompilerParams(collective_id=0, has_side_effects=True),
    )(fields[0], rod_coeffs, rod_mask, row, col)
    return out[None]


def solution(mesh):
    return jax.shard_map(
        functools.partial(local, mesh.shape["xy"], mesh.shape["guide"]),
        mesh=mesh,
        in_specs=(
            P("grp", "guide", "xy"),
            P(None, "guide", "xy"),
            P("guide", "xy"),
            P(),
            P("xy", None, None),
            P("xy", None, None),
            P("xy", None, None),
        ),
        out_specs=P("grp", "guide", "xy"),
        check_vma=False,
    )
```

```python
import functools

import jax
import jax.numpy as jnp
from jax import lax
from jax.experimental import pallas as pl
from jax.experimental.pallas import tpu as pltpu
from jax.sharding import PartitionSpec as P

S_ROD = 16
CY = 48
STEPS = 4
TILES_Y = 4

FLUID_A = 0.55
FLUID_B = 0.5
SOFT_SHARE = 0.35

LANES = 128
HALF = 64
CHUNK = 256
MESH = pl.DeviceIdType.MESH
F32 = jnp.float32
BF16 = jnp.bfloat16


def iota(shape, dim):
    return lax.broadcasted_iota(jnp.int32, shape, dim)


def split3(values):
    hi = values.astype(BF16)
    rest = values - hi.astype(F32)
    mid = rest.astype(BF16)
    low = (rest - mid.astype(F32)).astype(BF16)
    return jnp.concatenate([hi, mid, low], axis=0)


def join3(values):
    n = values.shape[0] // 3
    return values[:n] + values[n : 2 * n] + values[2 * n :]


def dot(a, b):
    return jnp.dot(a, b, preferred_element_type=F32)


def one_hot(cond):
    return jnp.where(cond, 1.0, 0.0).astype(BF16)


def kernel(
    n_xy,
    n_guide,
    f_hbm,
    c_hbm,
    m_hbm,
    counts_ref,
    fluid_ref,
    rod_ref,
    sides_ref,
    o_ref,
    c_ref,
    m_ref,
    in_sem,
    g_ref,
    s_ref,
    y_ref,
    mm_ref,
    lame_ref,
    shear_ref,
    be_ref,
    ebase_ref,
    send_i,
    recv_i,
    own_y,
    send_y,
    recv_yu,
    recv_yd,
    send_rim,
    recv_rim,
    send_x,
    recv_x,
    send_sem,
    recv_sem,
):
    levels, width = o_ref.shape
    rc = width // 9
    tc = width // 4
    rows = tc // CY
    tiles_x = n_xy // TILES_Y
    grp = lax.axis_index("grp")
    xy = lax.axis_index("xy")
    guide = lax.axis_index("guide")
    col_y = lax.rem(xy, TILES_Y)
    col_x = xy // TILES_Y
    feet = [(0, 0), (0, 1)] + ([(1, 0), (1, 1)] if tiles_x > 1 else [])
    nf = len(feet)
    up_g = lax.rem(guide + 1, n_guide)
    down_g = lax.rem(guide + n_guide - 1, n_guide)
    slots = fluid_ref.shape[2]
    bands = levels // 8
    half = levels // 2
    load_f = pltpu.make_async_copy(f_hbm, o_ref, in_sem.at[0])
    load_c = pltpu.make_async_copy(c_hbm, c_ref, in_sem.at[1])
    load_m = pltpu.make_async_copy(m_hbm, m_ref, in_sem.at[2])
    load_f.start()

    @pl.when(grp == 0)
    def _():
        load_c.start()
        load_m.start()

    YU, YD, RIM, XA, XB = nf, nf + 1, nf + 2, nf + 6, nf + 7

    def foot_has(o, solid):
        dx, dy = feet[o]
        if solid:
            return jnp.logical_and(col_y + dy < TILES_Y, col_x + dx < tiles_x)
        return jnp.logical_and(col_y >= dy, col_x >= dx)

    def foot_xy(o, solid):
        dx, dy = feet[o]
        off = dx * TILES_Y + dy
        return lax.rem(xy + off, n_xy) if solid else lax.rem(xy + n_xy - off, n_xy)

    def copy(src, dst, ch, s, device):
        return pltpu.make_async_remote_copy(
            src_ref=src,
            dst_ref=dst,
            send_sem=send_sem.at[ch, s],
            recv_sem=recv_sem.at[ch, s],
            device_id=device,
            device_id_type=MESH,
        )

    def c_foot(o, s, solid):
        return copy(
            send_i.at[s, o],
            recv_i.at[s, o],
            o,
            s,
            {"grp": 1 - grp, "xy": foot_xy(o, solid)},
        )

    def c_up(s):
        return copy(send_y.at[0, s], recv_yu.at[s], YU, s, {"xy": lax.rem(xy + n_xy - 1, n_xy)})

    def c_down(s):
        return copy(send_y.at[1, s], recv_yd.at[s], YD, s, {"xy": lax.rem(xy + 1, n_xy)})

    def c_rim(kind, s, size):
        cols = pl.ds(0, size)
        return copy(
            send_rim.at[kind, s, :, cols],
            recv_rim.at[kind, s, :, cols],
            RIM + kind,
            s,
            {"guide": down_g if kind % 2 else up_g},
        )

    def c_x(which, s):
        off = n_xy - TILES_Y if which == 0 else TILES_Y
        return copy(
            send_x.at[which, s],
            recv_x.at[which, s],
            XA + which,
            s,
            {"xy": lax.rem(xy + off, n_xy)},
        )

    has_next_y = col_y < TILES_Y - 1
    has_prev_y = col_y > 0
    has_next_x = col_x < tiles_x - 1
    has_prev_x = col_x > 0

    barrier = pltpu.get_barrier_semaphore()

    def greet(device):
        pl.semaphore_signal(barrier, inc=1, device_id=device, device_id_type=MESH)

    greet({"guide": up_g})
    greet({"guide": down_g})
    for solid in (True, False):
        for o in range(nf):
            mine = (grp == 0) if solid else (grp != 0)

            @pl.when(jnp.logical_and(mine, foot_has(o, solid)))
            def _():
                greet({"grp": 1 - grp, "xy": foot_xy(o, solid)})

    sides = [(has_next_y, 1), (has_prev_y, n_xy - 1)]
    if tiles_x > 1:
        sides += [(has_next_x, TILES_Y), (has_prev_x, n_xy - TILES_Y)]
    for has, off in sides:

        @pl.when(jnp.logical_and(grp != 0, has))
        def _():
            greet({"xy": lax.rem(xy + off, n_xy)})

    def as_int(cond):
        return jnp.where(cond, 1, 0)

    solid_n = sum(as_int(foot_has(o, True)) for o in range(nf))
    fluid_n = sum(as_int(foot_has(o, False)) for o in range(nf)) + sum(as_int(h) for h, _ in sides)
    expect = 2 + jnp.where(grp == 0, solid_n, fluid_n)

    lane = iota((levels, LANES), 1)
    lane8 = iota((8, LANES), 1)
    level8 = iota((8, 1), 0)
    spot = iota((LANES, 1), 0)
    pick = iota((LANES, slots), 1) == iota((LANES, slots), 0) % slots
    diagonal = iota((LANES, LANES), 0) == iota((LANES, LANES), 1)

    def as_column(table):
        wide = jnp.concatenate(
            [jnp.broadcast_to(table[o : o + 1, :], (slots, slots)) for o in range(LANES // slots)],
            axis=0,
        )
        return jnp.sum(jnp.where(pick, wide.astype(F32), 0.0), axis=1, keepdims=True)

    def as_row(column):
        return jnp.sum(jnp.where(diagonal, column, 0.0), axis=0, keepdims=True)

    def slot_columns(table, owner_of):
        column = as_column(table)
        row = as_row(column).astype(jnp.int32)
        column = column.astype(jnp.int32)
        count = jnp.zeros((LANES, 1), jnp.int32)
        for o in range(nf):
            count = jnp.where(spot // slots == o, counts_ref[owner_of(o), o], count)
        return row, jnp.where(spot % slots < count, column, -1)

    def pack(samples, o):
        out = pltpu.roll(samples[0:8], (-o * slots) % LANES, 1)
        for b in range(1, bands):
            moved = pltpu.roll(samples[8 * b : 8 * b + 8], ((b - o) * slots) % LANES, 1)
            out = jnp.where(lane8 >= b * slots, moved, out)
        return out

    def unfold(packed):
        return jnp.concatenate([packed, pltpu.roll(packed, HALF, 1)], axis=0)

    left = iota((half, LANES), 1) < HALF

    def comp(ref, member, size, r0):
        return ref[r0 : r0 + 8, member * size : (member + 1) * size]

    def lower(member, size, r0, rim):
        if r0 == 0:
            block = comp(o_ref, member, size, 0)
            return jnp.where(level8 == 0, rim, pltpu.roll(block, 1, 0))
        return o_ref[r0 - 1 : r0 + 7, member * size : (member + 1) * size]

    def upper(member, size, r0, rim):
        if r0 == levels - 8:
            block = comp(o_ref, member, size, r0)
            return jnp.where(level8 == 7, rim, pltpu.roll(block, 7, 0))
        return o_ref[r0 + 1 : r0 + 9, member * size : (member + 1) * size]

    def gather(start, size, lanes):
        acc = None
        for c in range(0, size, CHUNK):
            part = dot(
                split3(o_ref[:, start + c : start + c + CHUNK]),
                g_ref[c : c + CHUNK, lanes[0] : lanes[1]],
            )
            acc = part if acc is None else acc + part
        return join3(acc)

    def incoming(s):
        blocks = []
        for b in range(bands):
            block = pltpu.roll(recv_i[s, 0], (-b * slots) % LANES, 1)
            for o in range(1, nf):
                moved = pltpu.roll(recv_i[s, o], ((o - b) * slots) % LANES, 1)
                block = jnp.where(lane8 >= o * slots, moved, block)
            blocks.append(block)
        return jnp.where(lane < nf * slots, jnp.concatenate(blocks, axis=0), 0.0)

    def each_foot(solid, act):
        for o in range(nf):

            @pl.when(foot_has(o, solid))
            def _():
                act(o)

    def no_feet(solid):
        for o in range(1, nf):

            @pl.when(jnp.logical_not(foot_has(o, solid)))
            def _():
                recv_i[:, o] = jnp.zeros((STEPS, 8, LANES), F32)

    @pl.when(grp == 0)
    def _():
        no_feet(True)
        sides = sides_ref[0]
        row_idx, col_idx = slot_columns(sides // 2 * rc + rod_ref[0], lambda o: xy)
        facing = 2.0 * as_row(as_column(sides % 2)) - 1.0
        for c in range(0, 2 * rc, CHUNK):
            g_ref[c : c + CHUNK, 0:LANES] = one_hot(iota((CHUNK, LANES), 0) + c == row_idx)
            s_ref[0:LANES, c : c + CHUNK] = one_hot(iota((LANES, CHUNK), 1) + c == col_idx)
        mm_ref[0:LANES, 0:LANES] = one_hot(col_idx == row_idx)
        load_f.wait()

        def put_a(s):
            top = levels - 1
            send_rim[0, s, :, 0 : 2 * rc] = o_ref[top : top + 1, 7 * rc : 9 * rc]
            send_rim[1, s, :, 0:rc] = o_ref[0:1, 5 * rc : 6 * rc]
            c_rim(0, s, 2 * rc).start()
            c_rim(1, s, rc).start()

        pl.semaphore_wait(barrier, expect)
        put_a(0)
        load_c.wait()
        load_m.wait()
        for r0 in range(0, levels, 8):
            soft = jnp.where(m_ref[r0 : r0 + 8, :] == 1, 1.0, SOFT_SHARE).astype(F32)
            lame_ref[r0 : r0 + 8, :] = c_ref[0, r0 : r0 + 8, :] * soft
            shear_ref[r0 : r0 + 8, :] = c_ref[1, r0 : r0 + 8, :] * soft
        acc = None
        for c in range(0, 2 * rc, CHUNK):
            part = dot(
                split3(c_ref[2, :, c % rc : c % rc + CHUNK]), g_ref[c : c + CHUNK, 0:LANES]
            )
            acc = part if acc is None else acc + part
        be_ref[...] = join3(acc)

        place = iota((1, rc), 1)
        in_x = place // S_ROD % S_ROD
        in_y = place % S_ROD

        def fore_x(v):
            return jnp.where(in_x < S_ROD - 1, pltpu.roll(v, rc - S_ROD, 1), 0.0) - v

        def back_x(v):
            return v - jnp.where(in_x > 0, pltpu.roll(v, S_ROD, 1), 0.0)

        def fore_y(v):
            return jnp.where(in_y < S_ROD - 1, pltpu.roll(v, rc - 1, 1), 0.0) - v

        def back_y(v):
            return v - jnp.where(in_y > 0, pltpu.roll(v, 1, 1), 0.0)

        def store(member, r0, v):
            o_ref[r0 : r0 + 8, member * rc : (member + 1) * rc] = v

        def step(s, carry):
            c_rim(0, s, 2 * rc).wait_recv()
            c_rim(1, s, rc).wait_recv()
            for r0 in range(0, levels, 8):
                buo = c_ref[2, r0 : r0 + 8, :]
                xy_ = comp(o_ref, 6, rc, r0)
                xz = comp(o_ref, 7, rc, r0)
                yz = comp(o_ref, 8, rc, r0)
                xz_lo = lower(7, rc, r0, recv_rim[0, s, :, 0:rc])
                yz_lo = lower(8, rc, r0, recv_rim[0, s, :, rc : 2 * rc])
                store(
                    0,
                    r0,
                    comp(o_ref, 0, rc, r0)
                    + buo * (fore_x(comp(o_ref, 3, rc, r0)) + back_y(xy_) + (xz - xz_lo)),
                )
                store(
                    1,
                    r0,
                    comp(o_ref, 1, rc, r0)
                    + buo * (back_x(xy_) + fore_y(comp(o_ref, 4, rc, r0)) + (yz - yz_lo)),
                )
                zz = comp(o_ref, 5, rc, r0)
                zz_up = upper(5, rc, r0, recv_rim[1, s, :, 0:rc])
                store(
                    2,
                    r0,
                    comp(o_ref, 2, rc, r0) + buo * (back_x(xz) + back_y(yz) + (zz_up - zz)),
                )
            send_rim[2, s, :, 0:rc] = o_ref[levels - 1 : levels, 2 * rc : 3 * rc]
            c_rim(2, s, rc).start()
            base = gather(0, 2 * rc, (0, LANES))
            each_foot(True, lambda o: c_foot(o, s, True).wait_recv())
            lhs = split3(incoming(s) * (-facing))
            normal = base + be_ref[...] * join3(dot(lhs, mm_ref[0:LANES, 0:LANES]))
            normal = normal * facing
            for o in range(nf):
                send_i[s, o] = pack(normal, o)
            each_foot(True, lambda o: c_foot(o, s, True).start())
            for c in range(0, 2 * rc, CHUNK):
                push = join3(dot(lhs, s_ref[0:LANES, c : c + CHUNK]))
                o_ref[:, c : c + CHUNK] += c_ref[2, :, c % rc : c % rc + CHUNK] * push
            send_rim[3, s, :, 0 : 2 * rc] = o_ref[0:1, 0 : 2 * rc]
            c_rim(3, s, 2 * rc).start()
            c_rim(2, s, rc).wait_recv()
            c_rim(3, s, 2 * rc).wait_recv()
            for r0 in range(0, levels, 8):
                sx = comp(o_ref, 0, rc, r0)
                sy = comp(o_ref, 1, rc, r0)
                sz = comp(o_ref, 2, rc, r0)
                lame = lame_ref[r0 : r0 + 8, :]
                shear = shear_ref[r0 : r0 + 8, :]
                spread_x = back_x(sx)
                spread_y = back_y(sy)
                spread_z = sz - lower(2, rc, r0, recv_rim[2, s, :, 0:rc])
                bulk = lame * (spread_x + spread_y + spread_z)
                twice = 2.0 * shear
                store(3, r0, comp(o_ref, 3, rc, r0) + bulk + twice * spread_x)
                store(4, r0, comp(o_ref, 4, rc, r0) + bulk + twice * spread_y)
                store(5, r0, comp(o_ref, 5, rc, r0) + bulk + twice * spread_z)
                store(6, r0, comp(o_ref, 6, rc, r0) + shear * (fore_y(sx) + fore_x(sy)))
                sx_up = upper(0, rc, r0, recv_rim[3, s, :, 0:rc])
                sy_up = upper(1, rc, r0, recv_rim[3, s, :, rc : 2 * rc])
                store(7, r0, comp(o_ref, 7, rc, r0) + shear * (sx_up - sx + fore_x(sz)))
                store(8, r0, comp(o_ref, 8, rc, r0) + shear * (sy_up - sy + fore_y(sz)))

            @pl.when(s < STEPS - 1)
            def _():
                put_a(s + 1)

            return carry

        lax.fori_loop(0, STEPS, step, 0)

        def drain(s, carry):
            for kind, size in ((0, 2 * rc), (1, rc), (2, rc), (3, 2 * rc)):
                c_rim(kind, s, size).wait_send()
            each_foot(True, lambda o: c_foot(o, s, True).wait_send())
            return carry

        lax.fori_loop(0, STEPS, drain, 0)

    @pl.when(grp != 0)
    def _():
        no_feet(False)

        @pl.when(jnp.logical_not(has_next_y))
        def _():
            recv_yu[...] = jnp.zeros_like(recv_yu)

        @pl.when(jnp.logical_not(has_prev_y))
        def _():
            recv_yd[...] = jnp.zeros_like(recv_yd)

        if tiles_x > 1:

            @pl.when(jnp.logical_not(has_next_x))
            def _():
                recv_x[0] = jnp.zeros((STEPS, levels, LANES), F32)

            @pl.when(jnp.logical_not(has_prev_x))
            def _():
                recv_x[1] = jnp.zeros((STEPS, levels, LANES), F32)

        row_idx, col_idx = slot_columns(fluid_ref[0], lambda o: foot_xy(o, False))
        edge = iota((1, LANES), 1)
        edge_cols = jnp.where(
            edge < rows,
            edge * CY,
            jnp.where(
                jnp.logical_and(edge >= HALF, edge < HALF + rows),
                (edge - HALF) * CY + CY - 1,
                -2,
            ),
        )
        first_spots = jnp.where(spot < rows, spot * CY, -1)
        last_spots = jnp.where(spot < rows, spot * CY + CY - 1, -1)

        def put_rim(s):
            send_rim[1, s, :, 0:tc] = o_ref[0:1, 0:tc]
            c_rim(1, s, tc).start()
            if tiles_x > 1:
                send_x[0, s] = o_ref[:, 0:LANES]

                @pl.when(has_prev_x)
                def _():
                    c_x(0, s).start()

        def put_samples(s, both):
            samples = both[:, :LANES]
            for o in range(nf):
                send_i[s, o] = pack(samples, o)
            each_foot(False, lambda o: c_foot(o, s, False).start())
            edges = both[:, LANES:]
            own_y[...] = edges
            send_y[0, s] = jnp.where(left, edges[:half], pltpu.roll(edges[half:], HALF, 1))
            send_y[1, s] = jnp.where(left, pltpu.roll(edges[:half], HALF, 1), edges[half:])

            @pl.when(has_prev_y)
            def _():
                c_up(s).start()

            @pl.when(has_next_y)
            def _():
                c_down(s).start()

        for c in range(0, tc, CHUNK):
            g_ref[c : c + CHUNK, 0:LANES] = one_hot(iota((CHUNK, LANES), 0) + c == row_idx)
            g_ref[c : c + CHUNK, LANES:] = one_hot(iota((CHUNK, LANES), 0) + c == edge_cols)
        load_f.wait()
        pl.semaphore_wait(barrier, expect)
        put_samples(0, gather(0, tc, (0, 2 * LANES)))
        put_rim(0)
        flows = gather(2 * tc, tc, (LANES, 2 * LANES))
        send_y[1, STEPS] = jnp.where(left, pltpu.roll(flows[:half], HALF, 1), flows[half:])

        @pl.when(has_next_y)
        def _():
            c_down(STEPS).start()

        for c in range(0, tc, CHUNK):
            at = iota((LANES, CHUNK), 1) + c
            s_ref[0:LANES, c : c + CHUNK] = one_hot(at == col_idx)
            s_ref[LANES:, c : c + CHUNK] = one_hot(at == first_spots)
            y_ref[:, c : c + CHUNK] = one_hot(at == last_spots)
        mm_ref[0:LANES, 0:LANES] = one_hot(col_idx == row_idx)
        mm_ref[0:LANES, LANES:] = one_hot(col_idx == edge_cols)
        mm_ref[LANES:, 0:LANES] = one_hot(first_spots == row_idx)
        mm_ref[LANES:, LANES:] = one_hot(first_spots == edge_cols)

        @pl.when(has_prev_y)
        def _():
            c_down(STEPS).wait_recv()

        be_ref[...] = jnp.where(lane < rows, unfold(recv_yd[STEPS]), 0.0)

        place = iota((1, tc), 1)
        in_y = place % CY

        def store(member, r0, v):
            o_ref[r0 : r0 + 8, member * tc : (member + 1) * tc] = v

        def step(s, carry):
            c_rim(1, s, tc).wait_recv()
            if tiles_x > 1:

                @pl.when(has_next_x)
                def _():
                    c_x(0, s).wait_recv()

            for r0 in range(0, levels, 8):
                p = comp(o_ref, 0, tc, r0)
                next_x = jnp.where(place < tc - CY, pltpu.roll(p, tc - CY, 1), 0.0)
                store(1, r0, comp(o_ref, 1, tc, r0) - FLUID_B * (next_x - p))
                next_y = jnp.where(in_y < CY - 1, pltpu.roll(p, tc - 1, 1), 0.0)
                store(2, r0, comp(o_ref, 2, tc, r0) - FLUID_B * (next_y - p))
                next_z = upper(0, tc, r0, recv_rim[1, s, :, 0:tc])
                store(3, r0, comp(o_ref, 3, tc, r0) - FLUID_B * (next_z - p))
            send_rim[2, s, :, 0:tc] = o_ref[levels - 1 : levels, 3 * tc : 4 * tc]
            c_rim(2, s, tc).start()
            if tiles_x > 1:
                ahead = pltpu.roll(recv_x[0, s], LANES - CY, 1)
                tail = slice(2 * tc - LANES, 2 * tc)
                o_ref[:, tail] -= jnp.where(lane >= LANES - CY, FLUID_B * ahead, 0.0)
                send_x[1, s] = o_ref[:, tail]

                @pl.when(has_next_x)
                def _():
                    c_x(1, s).start()

            @pl.when(has_next_y)
            def _():
                c_up(s).wait_recv()

            @pl.when(has_prev_y)
            def _():
                c_down(s).wait_recv()

            lhs = split3(unfold(recv_yu[s]))
            for c in range(0, tc, CHUNK):
                o_ref[:, 2 * tc + c : 2 * tc + c + CHUNK] -= FLUID_B * join3(
                    dot(lhs, y_ref[:, c : c + CHUNK])
                )
            behind = be_ref[...] - FLUID_B * (own_y[...] - unfold(recv_yd[s]))
            behind = jnp.where(jnp.logical_and(lane < rows, has_prev_y), behind, 0.0)
            be_ref[...] = behind

            c_rim(2, s, tc).wait_recv()
            for r0 in range(0, levels, 8):
                fx = comp(o_ref, 1, tc, r0)
                fy = comp(o_ref, 2, tc, r0)
                fz = comp(o_ref, 3, tc, r0)
                prev_x = jnp.where(place >= CY, pltpu.roll(fx, CY, 1), 0.0)
                prev_y = jnp.where(in_y > 0, pltpu.roll(fy, 1, 1), 0.0)
                prev_z = lower(3, tc, r0, recv_rim[2, s, :, 0:tc])
                store(
                    0,
                    r0,
                    comp(o_ref, 0, tc, r0)
                    - FLUID_A * ((fx - prev_x) + (fy - prev_y) + (fz - prev_z)),
                )
            if tiles_x > 1:

                @pl.when(has_prev_x)
                def _():
                    c_x(1, s).wait_recv()

                before = pltpu.roll(recv_x[1, s], CY, 1)
                o_ref[:, 0:LANES] += jnp.where(lane < CY, FLUID_A * before, 0.0)

            @pl.when(s < STEPS - 1)
            def _():
                ebase_ref[...] = gather(0, tc, (0, 2 * LANES))

            each_foot(False, lambda o: c_foot(o, s, False).wait_recv())
            lhs = split3(jnp.concatenate([incoming(s), behind], axis=1))

            @pl.when(s < STEPS - 1)
            def _():
                put_samples(
                    s + 1, ebase_ref[...] + FLUID_A * join3(dot(lhs, mm_ref[...]))
                )

            for c in range(0, tc, CHUNK):
                o_ref[:, c : c + CHUNK] += FLUID_A * join3(dot(lhs, s_ref[:, c : c + CHUNK]))

            @pl.when(s < STEPS - 1)
            def _():
                put_rim(s + 1)

            return carry

        lax.fori_loop(0, STEPS, step, 0)

        def drain(s, carry):
            c_rim(1, s, tc).wait_send()
            c_rim(2, s, tc).wait_send()
            each_foot(False, lambda o: c_foot(o, s, False).wait_send())

            @pl.when(has_prev_y)
            def _():
                c_up(s).wait_send()

            @pl.when(has_next_y)
            def _():
                c_down(s).wait_send()

            if tiles_x > 1:

                @pl.when(has_prev_x)
                def _():
                    c_x(0, s).wait_send()

                @pl.when(has_next_x)
                def _():
                    c_x(1, s).wait_send()

            return carry

        lax.fori_loop(0, STEPS, drain, 0)

        @pl.when(has_next_y)
        def _():
            c_down(STEPS).wait_send()


def local(n_xy, n_guide, fields, rod_coeffs, rod_mask, pair_counts, fluid_slots, rod_slots, rod_sides):
    levels, width = fields.shape[1:]
    rc, tc = width // 9, width // 4
    n_feet = 4 if n_xy > TILES_Y else 2
    n_x = 2 if n_xy > TILES_Y else 1
    x_steps = STEPS if n_xy > TILES_Y else 1
    rim = max(2 * rc, tc)
    vmem = pl.BlockSpec(memory_space=pltpu.VMEM)
    smem = pl.BlockSpec(memory_space=pltpu.SMEM)
    hbm = pl.BlockSpec(memory_space=pl.ANY)
    out = pl.pallas_call(
        functools.partial(kernel, n_xy, n_guide),
        out_shape=pltpu.VMEM((levels, width), F32),
        in_specs=[hbm, hbm, hbm, smem, vmem, vmem, vmem],
        out_specs=vmem,
        scratch_shapes=[
            pltpu.VMEM((3, levels, rc), F32),
            pltpu.VMEM((levels, rc), jnp.int32),
            pltpu.SemaphoreType.DMA((3,)),
            pltpu.VMEM((tc, 2 * LANES), BF16),
            pltpu.VMEM((2 * LANES, tc), BF16),
            pltpu.VMEM((LANES, tc), BF16),
            pltpu.VMEM((2 * LANES, 2 * LANES), BF16),
            pltpu.VMEM((levels, rc), F32),
            pltpu.VMEM((levels, rc), F32),
            pltpu.VMEM((levels, LANES), F32),
            pltpu.VMEM((levels, 2 * LANES), F32),
            pltpu.VMEM((STEPS, n_feet, 8, LANES), F32),
            pltpu.VMEM((STEPS, n_feet, 8, LANES), F32),
            pltpu.VMEM((levels, LANES), F32),
            pltpu.VMEM((2, STEPS + 1, levels // 2, LANES), F32),
            pltpu.VMEM((STEPS + 1, levels // 2, LANES), F32),
            pltpu.VMEM((STEPS + 1, levels // 2, LANES), F32),
            pltpu.VMEM((4, STEPS, 1, rim), F32),
            pltpu.VMEM((4, STEPS, 1, rim), F32),
            pltpu.VMEM((n_x, x_steps, levels, LANES), F32),
            pltpu.VMEM((n_x, x_steps, levels, LANES), F32),
            pltpu.SemaphoreType.DMA((n_feet + 8, STEPS + 1)),
            pltpu.SemaphoreType.DMA((n_feet + 8, STEPS + 1)),
        ],
        compiler_params=pltpu.CompilerParams(collective_id=0, has_side_effects=True),
    )(fields[0], rod_coeffs, rod_mask, pair_counts, fluid_slots, rod_slots, rod_sides)
    return out[None]


def solution(mesh):
    return jax.shard_map(
        functools.partial(local, mesh.shape["xy"], mesh.shape["guide"]),
        mesh=mesh,
        in_specs=(
            P("grp", "guide", "xy"),
            P(None, "guide", "xy"),
            P("guide", "xy"),
            P(),
            P("xy", None, None),
            P("xy", None, None),
            P("xy", None, None),
        ),
        out_specs=P("grp", "guide", "xy"),
        check_vma=False,
    )
```

```python
import functools

import jax
import jax.numpy as jnp
from jax import lax
from jax.experimental import pallas as pl
from jax.experimental.pallas import tpu as pltpu
from jax.sharding import PartitionSpec as P

S_ROD = 16
CY = 48
STEPS = 4
TILES_Y = 4

FLUID_A = 0.55
FLUID_B = 0.5
SOFT_SHARE = 0.35

LANES = 128
HALF = 64
CHUNK = 256
MESH = pl.DeviceIdType.MESH
F32 = jnp.float32
BF16 = jnp.bfloat16


def iota(shape, dim):
    return lax.broadcasted_iota(jnp.int32, shape, dim)


def split3(values):
    hi = values.astype(BF16)
    rest = values - hi.astype(F32)
    mid = rest.astype(BF16)
    low = (rest - mid.astype(F32)).astype(BF16)
    return jnp.concatenate([hi, mid, low], axis=0)


def join3(values):
    n = values.shape[0] // 3
    return values[:n] + values[n : 2 * n] + values[2 * n :]


def dot(a, b):
    return jnp.dot(a, b, preferred_element_type=F32)


def one_hot(cond):
    return jnp.where(cond, 1.0, 0.0).astype(BF16)


def kernel(
    n_xy,
    n_guide,
    f_hbm,
    c_hbm,
    m_hbm,
    counts_ref,
    fluid_ref,
    rod_ref,
    sides_ref,
    o_ref,
    c_ref,
    m_ref,
    in_sem,
    g_ref,
    s_ref,
    y_ref,
    mm_ref,
    lame_ref,
    shear_ref,
    be_ref,
    ebase_ref,
    send_i,
    recv_i,
    own_y,
    send_y,
    recv_yu,
    recv_yd,
    send_rim,
    recv_rim,
    send_x,
    recv_x,
    send_sem,
    recv_sem,
):
    levels, width = o_ref.shape
    rc = width // 9
    tc = width // 4
    rows = tc // CY
    tiles_x = n_xy // TILES_Y
    grp = lax.axis_index("grp")
    xy = lax.axis_index("xy")
    guide = lax.axis_index("guide")
    col_y = lax.rem(xy, TILES_Y)
    col_x = xy // TILES_Y
    feet = [(0, 0), (0, 1)] + ([(1, 0), (1, 1)] if tiles_x > 1 else [])
    nf = len(feet)
    up_g = lax.rem(guide + 1, n_guide)
    down_g = lax.rem(guide + n_guide - 1, n_guide)
    slots = fluid_ref.shape[2]
    bands = levels // 8
    half = levels // 2
    load_f = pltpu.make_async_copy(f_hbm, o_ref, in_sem.at[0])
    load_c = pltpu.make_async_copy(c_hbm, c_ref, in_sem.at[1])
    load_m = pltpu.make_async_copy(m_hbm, m_ref, in_sem.at[2])
    load_f.start()

    @pl.when(grp == 0)
    def _():
        load_c.start()
        load_m.start()

    YU, YD, RIM, XA, XB = nf, nf + 1, nf + 2, nf + 6, nf + 7

    def foot_has(o, solid):
        dx, dy = feet[o]
        if solid:
            return jnp.logical_and(col_y + dy < TILES_Y, col_x + dx < tiles_x)
        return jnp.logical_and(col_y >= dy, col_x >= dx)

    def foot_xy(o, solid):
        dx, dy = feet[o]
        off = dx * TILES_Y + dy
        return lax.rem(xy + off, n_xy) if solid else lax.rem(xy + n_xy - off, n_xy)

    def copy(src, dst, ch, s, device):
        return pltpu.make_async_remote_copy(
            src_ref=src,
            dst_ref=dst,
            send_sem=send_sem.at[ch, s],
            recv_sem=recv_sem.at[ch, s],
            device_id=device,
            device_id_type=MESH,
        )

    def c_foot(o, s, solid):
        return copy(
            send_i.at[s, o],
            recv_i.at[s, o],
            o,
            s,
            {"grp": 1 - grp, "xy": foot_xy(o, solid)},
        )

    def c_up(s):
        return copy(send_y.at[0, s], recv_yu.at[s], YU, s, {"xy": lax.rem(xy + n_xy - 1, n_xy)})

    def c_down(s):
        return copy(send_y.at[1, s], recv_yd.at[s], YD, s, {"xy": lax.rem(xy + 1, n_xy)})

    def c_rim(kind, s, size):
        cols = pl.ds(0, size)
        return copy(
            send_rim.at[kind, s, :, cols],
            recv_rim.at[kind, s, :, cols],
            RIM + kind,
            s,
            {"guide": down_g if kind % 2 else up_g},
        )

    def c_x(which, s):
        off = n_xy - TILES_Y if which == 0 else TILES_Y
        return copy(
            send_x.at[which, s],
            recv_x.at[which, s],
            XA + which,
            s,
            {"xy": lax.rem(xy + off, n_xy)},
        )

    has_next_y = col_y < TILES_Y - 1
    has_prev_y = col_y > 0
    has_next_x = col_x < tiles_x - 1
    has_prev_x = col_x > 0

    barrier = pltpu.get_barrier_semaphore()

    def greet(device):
        pl.semaphore_signal(barrier, inc=1, device_id=device, device_id_type=MESH)

    greet({"guide": up_g})
    greet({"guide": down_g})
    for solid in (True, False):
        for o in range(nf):
            mine = (grp == 0) if solid else (grp != 0)

            @pl.when(jnp.logical_and(mine, foot_has(o, solid)))
            def _():
                greet({"grp": 1 - grp, "xy": foot_xy(o, solid)})

    sides = [(has_next_y, 1), (has_prev_y, n_xy - 1)]
    if tiles_x > 1:
        sides += [(has_next_x, TILES_Y), (has_prev_x, n_xy - TILES_Y)]
    for has, off in sides:

        @pl.when(jnp.logical_and(grp != 0, has))
        def _():
            greet({"xy": lax.rem(xy + off, n_xy)})

    def as_int(cond):
        return jnp.where(cond, 1, 0)

    solid_n = sum(as_int(foot_has(o, True)) for o in range(nf))
    fluid_n = sum(as_int(foot_has(o, False)) for o in range(nf)) + sum(as_int(h) for h, _ in sides)
    expect = 2 + jnp.where(grp == 0, solid_n, fluid_n)

    lane = iota((levels, LANES), 1)
    lane8 = iota((8, LANES), 1)
    level8 = iota((8, 1), 0)
    spot = iota((LANES, 1), 0)
    pick = iota((LANES, slots), 1) == iota((LANES, slots), 0) % slots
    diagonal = iota((LANES, LANES), 0) == iota((LANES, LANES), 1)

    def as_column(table):
        wide = jnp.concatenate(
            [jnp.broadcast_to(table[o : o + 1, :], (slots, slots)) for o in range(LANES // slots)],
            axis=0,
        )
        return jnp.sum(jnp.where(pick, wide.astype(F32), 0.0), axis=1, keepdims=True)

    def as_row(column):
        return jnp.sum(jnp.where(diagonal, column, 0.0), axis=0, keepdims=True)

    def slot_columns(table, owner_of):
        column = as_column(table)
        row = as_row(column).astype(jnp.int32)
        column = column.astype(jnp.int32)
        count = jnp.zeros((LANES, 1), jnp.int32)
        for o in range(nf):
            count = jnp.where(spot // slots == o, counts_ref[owner_of(o), o], count)
        return row, jnp.where(spot % slots < count, column, -1)

    def pack(samples, o):
        out = pltpu.roll(samples[0:8], (-o * slots) % LANES, 1)
        for b in range(1, bands):
            moved = pltpu.roll(samples[8 * b : 8 * b + 8], ((b - o) * slots) % LANES, 1)
            out = jnp.where(lane8 >= b * slots, moved, out)
        return out

    def unfold(packed):
        return jnp.concatenate([packed, pltpu.roll(packed, HALF, 1)], axis=0)

    left = iota((half, LANES), 1) < HALF

    def comp(ref, member, size, r0):
        return ref[r0 : r0 + 8, member * size : (member + 1) * size]

    def lower(member, size, r0, rim):
        if r0 == 0:
            block = comp(o_ref, member, size, 0)
            return jnp.where(level8 == 0, rim, pltpu.roll(block, 1, 0))
        return o_ref[r0 - 1 : r0 + 7, member * size : (member + 1) * size]

    def upper(member, size, r0, rim):
        if r0 == levels - 8:
            block = comp(o_ref, member, size, r0)
            return jnp.where(level8 == 7, rim, pltpu.roll(block, 7, 0))
        return o_ref[r0 + 1 : r0 + 9, member * size : (member + 1) * size]

    def gather(start, size, lanes):
        acc = None
        for c in range(0, size, CHUNK):
            part = dot(
                split3(o_ref[:, start + c : start + c + CHUNK]),
                g_ref[c : c + CHUNK, lanes[0] : lanes[1]],
            )
            acc = part if acc is None else acc + part
        return join3(acc)

    def incoming(s):
        blocks = []
        for b in range(bands):
            block = pltpu.roll(recv_i[s, 0], (-b * slots) % LANES, 1)
            for o in range(1, nf):
                moved = pltpu.roll(recv_i[s, o], ((o - b) * slots) % LANES, 1)
                block = jnp.where(lane8 >= o * slots, moved, block)
            blocks.append(block)
        return jnp.where(lane < nf * slots, jnp.concatenate(blocks, axis=0), 0.0)

    def each_foot(solid, act):
        for o in range(nf):

            @pl.when(foot_has(o, solid))
            def _():
                act(o)

    def no_feet(solid):
        for o in range(1, nf):

            @pl.when(jnp.logical_not(foot_has(o, solid)))
            def _():
                recv_i[:, o] = jnp.zeros((STEPS, 8, LANES), F32)

    @pl.when(grp == 0)
    def _():
        no_feet(True)
        sides = sides_ref[0]
        row_idx, col_idx = slot_columns(sides // 2 * rc + rod_ref[0], lambda o: xy)
        facing = 2.0 * as_row(as_column(sides % 2)) - 1.0
        for c in range(0, 2 * rc, CHUNK):
            g_ref[c : c + CHUNK, 0:LANES] = one_hot(iota((CHUNK, LANES), 0) + c == row_idx)
            s_ref[0:LANES, c : c + CHUNK] = one_hot(iota((LANES, CHUNK), 1) + c == col_idx)
        mm_ref[0:LANES, 0:LANES] = one_hot(col_idx == row_idx)
        load_f.wait()

        def put_under(s):
            top = levels - 1
            send_rim[0, s, :, 0 : 2 * rc] = o_ref[top : top + 1, 7 * rc : 9 * rc]
            c_rim(0, s, 2 * rc).start()

        def put_over(s):
            send_rim[1, s, :, 0:rc] = o_ref[0:1, 5 * rc : 6 * rc]
            c_rim(1, s, rc).start()

        pl.semaphore_wait(barrier, expect)
        put_over(0)
        put_under(0)
        load_c.wait()
        load_m.wait()
        for r0 in range(0, levels, 8):
            soft = jnp.where(m_ref[r0 : r0 + 8, :] == 1, 1.0, SOFT_SHARE).astype(F32)
            lame_ref[r0 : r0 + 8, :] = c_ref[0, r0 : r0 + 8, :] * soft
            shear_ref[r0 : r0 + 8, :] = c_ref[1, r0 : r0 + 8, :] * soft
        acc = None
        for c in range(0, 2 * rc, CHUNK):
            part = dot(
                split3(c_ref[2, :, c % rc : c % rc + CHUNK]), g_ref[c : c + CHUNK, 0:LANES]
            )
            acc = part if acc is None else acc + part
        be_ref[...] = join3(acc)

        place = iota((1, rc), 1)
        in_x = place // S_ROD % S_ROD
        in_y = place % S_ROD

        def fore_x(v):
            return jnp.where(in_x < S_ROD - 1, pltpu.roll(v, rc - S_ROD, 1), 0.0) - v

        def back_x(v):
            return v - jnp.where(in_x > 0, pltpu.roll(v, S_ROD, 1), 0.0)

        def fore_y(v):
            return jnp.where(in_y < S_ROD - 1, pltpu.roll(v, rc - 1, 1), 0.0) - v

        def back_y(v):
            return v - jnp.where(in_y > 0, pltpu.roll(v, 1, 1), 0.0)

        def store(member, r0, v):
            o_ref[r0 : r0 + 8, member * rc : (member + 1) * rc] = v

        def step(s, carry):
            for r0 in [*range(8, levels, 8), 0]:
                if r0 == levels - 8:
                    c_rim(1, s, rc).wait_recv()
                if r0 == 0:
                    c_rim(0, s, 2 * rc).wait_recv()
                buo = c_ref[2, r0 : r0 + 8, :]
                xy_ = comp(o_ref, 6, rc, r0)
                xz = comp(o_ref, 7, rc, r0)
                yz = comp(o_ref, 8, rc, r0)
                xz_lo = lower(7, rc, r0, recv_rim[0, s, :, 0:rc])
                yz_lo = lower(8, rc, r0, recv_rim[0, s, :, rc : 2 * rc])
                store(
                    0,
                    r0,
                    comp(o_ref, 0, rc, r0)
                    + buo * (fore_x(comp(o_ref, 3, rc, r0)) + back_y(xy_) + (xz - xz_lo)),
                )
                store(
                    1,
                    r0,
                    comp(o_ref, 1, rc, r0)
                    + buo * (back_x(xy_) + fore_y(comp(o_ref, 4, rc, r0)) + (yz - yz_lo)),
                )
                zz = comp(o_ref, 5, rc, r0)
                zz_up = upper(5, rc, r0, recv_rim[1, s, :, 0:rc])
                store(
                    2,
                    r0,
                    comp(o_ref, 2, rc, r0) + buo * (back_x(xz) + back_y(yz) + (zz_up - zz)),
                )
                if r0 == levels - 8:
                    send_rim[2, s, :, 0:rc] = o_ref[levels - 1 : levels, 2 * rc : 3 * rc]
                    c_rim(2, s, rc).start()
            base = gather(0, 2 * rc, (0, LANES))
            each_foot(True, lambda o: c_foot(o, s, True).wait_recv())
            lhs = split3(incoming(s) * (-facing))
            normal = base + be_ref[...] * join3(dot(lhs, mm_ref[0:LANES, 0:LANES]))
            normal = normal * facing
            for o in range(nf):
                send_i[s, o] = pack(normal, o)
            each_foot(True, lambda o: c_foot(o, s, True).start())
            for c in range(0, 2 * rc, CHUNK):
                push = join3(dot(lhs, s_ref[0:LANES, c : c + CHUNK]))
                o_ref[:, c : c + CHUNK] += c_ref[2, :, c % rc : c % rc + CHUNK] * push
            send_rim[3, s, :, 0 : 2 * rc] = o_ref[0:1, 0 : 2 * rc]
            c_rim(3, s, 2 * rc).start()
            for r0 in [*range(8, levels - 8, 8), 0, levels - 8]:
                if r0 == 0:
                    c_rim(2, s, rc).wait_recv()
                if r0 == levels - 8:
                    c_rim(3, s, 2 * rc).wait_recv()
                sx = comp(o_ref, 0, rc, r0)
                sy = comp(o_ref, 1, rc, r0)
                sz = comp(o_ref, 2, rc, r0)
                lame = lame_ref[r0 : r0 + 8, :]
                shear = shear_ref[r0 : r0 + 8, :]
                spread_x = back_x(sx)
                spread_y = back_y(sy)
                spread_z = sz - lower(2, rc, r0, recv_rim[2, s, :, 0:rc])
                bulk = lame * (spread_x + spread_y + spread_z)
                twice = 2.0 * shear
                store(3, r0, comp(o_ref, 3, rc, r0) + bulk + twice * spread_x)
                store(4, r0, comp(o_ref, 4, rc, r0) + bulk + twice * spread_y)
                store(5, r0, comp(o_ref, 5, rc, r0) + bulk + twice * spread_z)
                store(6, r0, comp(o_ref, 6, rc, r0) + shear * (fore_y(sx) + fore_x(sy)))
                sx_up = upper(0, rc, r0, recv_rim[3, s, :, 0:rc])
                sy_up = upper(1, rc, r0, recv_rim[3, s, :, rc : 2 * rc])
                store(7, r0, comp(o_ref, 7, rc, r0) + shear * (sx_up - sx + fore_x(sz)))
                store(8, r0, comp(o_ref, 8, rc, r0) + shear * (sy_up - sy + fore_y(sz)))
                if r0 == 0:

                    @pl.when(s < STEPS - 1)
                    def _():
                        put_over(s + 1)

            @pl.when(s < STEPS - 1)
            def _():
                put_under(s + 1)

            return carry

        lax.fori_loop(0, STEPS, step, 0)

        def drain(s, carry):
            for kind, size in ((0, 2 * rc), (1, rc), (2, rc), (3, 2 * rc)):
                c_rim(kind, s, size).wait_send()
            each_foot(True, lambda o: c_foot(o, s, True).wait_send())
            return carry

        lax.fori_loop(0, STEPS, drain, 0)

    @pl.when(grp != 0)
    def _():
        no_feet(False)

        @pl.when(jnp.logical_not(has_next_y))
        def _():
            recv_yu[...] = jnp.zeros_like(recv_yu)

        @pl.when(jnp.logical_not(has_prev_y))
        def _():
            recv_yd[...] = jnp.zeros_like(recv_yd)

        if tiles_x > 1:

            @pl.when(jnp.logical_not(has_next_x))
            def _():
                recv_x[0] = jnp.zeros((STEPS, levels, LANES), F32)

            @pl.when(jnp.logical_not(has_prev_x))
            def _():
                recv_x[1] = jnp.zeros((STEPS, levels, LANES), F32)

        row_idx, col_idx = slot_columns(fluid_ref[0], lambda o: foot_xy(o, False))
        edge = iota((1, LANES), 1)
        edge_cols = jnp.where(
            edge < rows,
            edge * CY,
            jnp.where(
                jnp.logical_and(edge >= HALF, edge < HALF + rows),
                (edge - HALF) * CY + CY - 1,
                -2,
            ),
        )
        first_spots = jnp.where(spot < rows, spot * CY, -1)
        last_spots = jnp.where(spot < rows, spot * CY + CY - 1, -1)

        def put_rim(s):
            send_rim[1, s, :, 0:tc] = o_ref[0:1, 0:tc]
            c_rim(1, s, tc).start()
            if tiles_x > 1:
                send_x[0, s] = o_ref[:, 0:LANES]

                @pl.when(has_prev_x)
                def _():
                    c_x(0, s).start()

        def put_samples(s, both):
            samples = both[:, :LANES]
            for o in range(nf):
                send_i[s, o] = pack(samples, o)
            each_foot(False, lambda o: c_foot(o, s, False).start())
            edges = both[:, LANES:]
            own_y[...] = edges
            send_y[0, s] = jnp.where(left, edges[:half], pltpu.roll(edges[half:], HALF, 1))
            send_y[1, s] = jnp.where(left, pltpu.roll(edges[:half], HALF, 1), edges[half:])

            @pl.when(has_prev_y)
            def _():
                c_up(s).start()

            @pl.when(has_next_y)
            def _():
                c_down(s).start()

        for c in range(0, tc, CHUNK):
            g_ref[c : c + CHUNK, 0:LANES] = one_hot(iota((CHUNK, LANES), 0) + c == row_idx)
            g_ref[c : c + CHUNK, LANES:] = one_hot(iota((CHUNK, LANES), 0) + c == edge_cols)
        load_f.wait()
        pl.semaphore_wait(barrier, expect)
        put_samples(0, gather(0, tc, (0, 2 * LANES)))
        put_rim(0)
        flows = gather(2 * tc, tc, (LANES, 2 * LANES))
        send_y[1, STEPS] = jnp.where(left, pltpu.roll(flows[:half], HALF, 1), flows[half:])

        @pl.when(has_next_y)
        def _():
            c_down(STEPS).start()

        for c in range(0, tc, CHUNK):
            at = iota((LANES, CHUNK), 1) + c
            s_ref[0:LANES, c : c + CHUNK] = one_hot(at == col_idx)
            s_ref[LANES:, c : c + CHUNK] = one_hot(at == first_spots)
            y_ref[:, c : c + CHUNK] = one_hot(at == last_spots)
        mm_ref[0:LANES, 0:LANES] = one_hot(col_idx == row_idx)
        mm_ref[0:LANES, LANES:] = one_hot(col_idx == edge_cols)
        mm_ref[LANES:, 0:LANES] = one_hot(first_spots == row_idx)
        mm_ref[LANES:, LANES:] = one_hot(first_spots == edge_cols)

        @pl.when(has_prev_y)
        def _():
            c_down(STEPS).wait_recv()

        be_ref[...] = jnp.where(lane < rows, unfold(recv_yd[STEPS]), 0.0)

        place = iota((1, tc), 1)
        in_y = place % CY

        def store(member, r0, v):
            o_ref[r0 : r0 + 8, member * tc : (member + 1) * tc] = v

        def step(s, carry):
            for r0 in range(0, levels, 8):
                if r0 == levels - 8:
                    c_rim(1, s, tc).wait_recv()
                p = comp(o_ref, 0, tc, r0)
                next_x = jnp.where(place < tc - CY, pltpu.roll(p, tc - CY, 1), 0.0)
                store(1, r0, comp(o_ref, 1, tc, r0) - FLUID_B * (next_x - p))
                next_y = jnp.where(in_y < CY - 1, pltpu.roll(p, tc - 1, 1), 0.0)
                store(2, r0, comp(o_ref, 2, tc, r0) - FLUID_B * (next_y - p))
                next_z = upper(0, tc, r0, recv_rim[1, s, :, 0:tc])
                store(3, r0, comp(o_ref, 3, tc, r0) - FLUID_B * (next_z - p))
            send_rim[2, s, :, 0:tc] = o_ref[levels - 1 : levels, 3 * tc : 4 * tc]
            c_rim(2, s, tc).start()
            if tiles_x > 1:

                @pl.when(has_next_x)
                def _():
                    c_x(0, s).wait_recv()

                ahead = pltpu.roll(recv_x[0, s], LANES - CY, 1)
                tail = slice(2 * tc - LANES, 2 * tc)
                o_ref[:, tail] -= jnp.where(lane >= LANES - CY, FLUID_B * ahead, 0.0)
                send_x[1, s] = o_ref[:, tail]

                @pl.when(has_next_x)
                def _():
                    c_x(1, s).start()

            @pl.when(has_next_y)
            def _():
                c_up(s).wait_recv()

            @pl.when(has_prev_y)
            def _():
                c_down(s).wait_recv()

            lhs = split3(unfold(recv_yu[s]))
            for c in range(0, tc, CHUNK):
                o_ref[:, 2 * tc + c : 2 * tc + c + CHUNK] -= FLUID_B * join3(
                    dot(lhs, y_ref[:, c : c + CHUNK])
                )
            behind = be_ref[...] - FLUID_B * (own_y[...] - unfold(recv_yd[s]))
            behind = jnp.where(jnp.logical_and(lane < rows, has_prev_y), behind, 0.0)
            be_ref[...] = behind

            for r0 in [*range(8, levels, 8), 0]:
                if r0 == 0:
                    c_rim(2, s, tc).wait_recv()
                fx = comp(o_ref, 1, tc, r0)
                fy = comp(o_ref, 2, tc, r0)
                fz = comp(o_ref, 3, tc, r0)
                prev_x = jnp.where(place >= CY, pltpu.roll(fx, CY, 1), 0.0)
                prev_y = jnp.where(in_y > 0, pltpu.roll(fy, 1, 1), 0.0)
                prev_z = lower(3, tc, r0, recv_rim[2, s, :, 0:tc])
                store(
                    0,
                    r0,
                    comp(o_ref, 0, tc, r0)
                    - FLUID_A * ((fx - prev_x) + (fy - prev_y) + (fz - prev_z)),
                )
            if tiles_x > 1:

                @pl.when(has_prev_x)
                def _():
                    c_x(1, s).wait_recv()

                before = pltpu.roll(recv_x[1, s], CY, 1)
                o_ref[:, 0:LANES] += jnp.where(lane < CY, FLUID_A * before, 0.0)

            @pl.when(s < STEPS - 1)
            def _():
                ebase_ref[...] = gather(0, tc, (0, 2 * LANES))

            each_foot(False, lambda o: c_foot(o, s, False).wait_recv())
            lhs = split3(jnp.concatenate([incoming(s), behind], axis=1))

            @pl.when(s < STEPS - 1)
            def _():
                put_samples(
                    s + 1, ebase_ref[...] + FLUID_A * join3(dot(lhs, mm_ref[...]))
                )

            for c in range(0, tc, CHUNK):
                o_ref[:, c : c + CHUNK] += FLUID_A * join3(dot(lhs, s_ref[:, c : c + CHUNK]))

            @pl.when(s < STEPS - 1)
            def _():
                put_rim(s + 1)

            return carry

        lax.fori_loop(0, STEPS, step, 0)

        def drain(s, carry):
            c_rim(1, s, tc).wait_send()
            c_rim(2, s, tc).wait_send()
            each_foot(False, lambda o: c_foot(o, s, False).wait_send())

            @pl.when(has_prev_y)
            def _():
                c_up(s).wait_send()

            @pl.when(has_next_y)
            def _():
                c_down(s).wait_send()

            if tiles_x > 1:

                @pl.when(has_prev_x)
                def _():
                    c_x(0, s).wait_send()

                @pl.when(has_next_x)
                def _():
                    c_x(1, s).wait_send()

            return carry

        lax.fori_loop(0, STEPS, drain, 0)

        @pl.when(has_next_y)
        def _():
            c_down(STEPS).wait_send()


def local(n_xy, n_guide, fields, rod_coeffs, rod_mask, pair_counts, fluid_slots, rod_slots, rod_sides):
    levels, width = fields.shape[1:]
    rc, tc = width // 9, width // 4
    n_feet = 4 if n_xy > TILES_Y else 2
    n_x = 2 if n_xy > TILES_Y else 1
    x_steps = STEPS if n_xy > TILES_Y else 1
    rim = max(2 * rc, tc)
    vmem = pl.BlockSpec(memory_space=pltpu.VMEM)
    smem = pl.BlockSpec(memory_space=pltpu.SMEM)
    hbm = pl.BlockSpec(memory_space=pl.ANY)
    out = pl.pallas_call(
        functools.partial(kernel, n_xy, n_guide),
        out_shape=pltpu.VMEM((levels, width), F32),
        in_specs=[hbm, hbm, hbm, smem, vmem, vmem, vmem],
        out_specs=vmem,
        scratch_shapes=[
            pltpu.VMEM((3, levels, rc), F32),
            pltpu.VMEM((levels, rc), jnp.int32),
            pltpu.SemaphoreType.DMA((3,)),
            pltpu.VMEM((tc, 2 * LANES), BF16),
            pltpu.VMEM((2 * LANES, tc), BF16),
            pltpu.VMEM((LANES, tc), BF16),
            pltpu.VMEM((2 * LANES, 2 * LANES), BF16),
            pltpu.VMEM((levels, rc), F32),
            pltpu.VMEM((levels, rc), F32),
            pltpu.VMEM((levels, LANES), F32),
            pltpu.VMEM((levels, 2 * LANES), F32),
            pltpu.VMEM((STEPS, n_feet, 8, LANES), F32),
            pltpu.VMEM((STEPS, n_feet, 8, LANES), F32),
            pltpu.VMEM((levels, LANES), F32),
            pltpu.VMEM((2, STEPS + 1, levels // 2, LANES), F32),
            pltpu.VMEM((STEPS + 1, levels // 2, LANES), F32),
            pltpu.VMEM((STEPS + 1, levels // 2, LANES), F32),
            pltpu.VMEM((4, STEPS, 1, rim), F32),
            pltpu.VMEM((4, STEPS, 1, rim), F32),
            pltpu.VMEM((n_x, x_steps, levels, LANES), F32),
            pltpu.VMEM((n_x, x_steps, levels, LANES), F32),
            pltpu.SemaphoreType.DMA((n_feet + 8, STEPS + 1)),
            pltpu.SemaphoreType.DMA((n_feet + 8, STEPS + 1)),
        ],
        compiler_params=pltpu.CompilerParams(collective_id=0, has_side_effects=True),
    )(fields[0], rod_coeffs, rod_mask, pair_counts, fluid_slots, rod_slots, rod_sides)
    return out[None]


def solution(mesh):
    return jax.shard_map(
        functools.partial(local, mesh.shape["xy"], mesh.shape["guide"]),
        mesh=mesh,
        in_specs=(
            P("grp", "guide", "xy"),
            P(None, "guide", "xy"),
            P("guide", "xy"),
            P(),
            P("xy", None, None),
            P("xy", None, None),
            P("xy", None, None),
        ),
        out_specs=P("grp", "guide", "xy"),
        check_vma=False,
    )
```

```python
import functools

import jax
import jax.numpy as jnp
from jax import lax
from jax.experimental import pallas as pl
from jax.experimental.pallas import tpu as pltpu
from jax.sharding import PartitionSpec as P

S_ROD = 16
CY = 48
STEPS = 4
TILES_Y = 4

FLUID_A = 0.55
FLUID_B = 0.5
SOFT_SHARE = 0.35

LANES = 128
HALF = 64
CHUNK = 256
MESH = pl.DeviceIdType.MESH
F32 = jnp.float32
BF16 = jnp.bfloat16


def iota(shape, dim):
    return lax.broadcasted_iota(jnp.int32, shape, dim)


def split3(values):
    hi = values.astype(BF16)
    rest = values - hi.astype(F32)
    mid = rest.astype(BF16)
    low = (rest - mid.astype(F32)).astype(BF16)
    return jnp.concatenate([hi, mid, low], axis=0)


def join3(values):
    n = values.shape[0] // 3
    return values[:n] + values[n : 2 * n] + values[2 * n :]


def dot(a, b):
    return jnp.dot(a, b, preferred_element_type=F32)


def one_hot(cond):
    return jnp.where(cond, 1.0, 0.0).astype(BF16)


def kernel(
    n_xy,
    n_guide,
    f_hbm,
    c_hbm,
    m_hbm,
    counts_ref,
    fluid_ref,
    rod_ref,
    sides_ref,
    o_ref,
    c_ref,
    m_ref,
    in_sem,
    g_ref,
    s_ref,
    y_ref,
    mm_ref,
    lame_ref,
    shear_ref,
    be_ref,
    ebase_ref,
    send_i,
    recv_i,
    own_y,
    send_y,
    recv_yu,
    recv_yd,
    send_rim,
    recv_rim,
    send_x,
    recv_x,
    send_sem,
    recv_sem,
):
    levels, width = o_ref.shape
    rc = width // 9
    tc = width // 4
    rows = tc // CY
    tiles_x = n_xy // TILES_Y
    grp = lax.axis_index("grp")
    xy = lax.axis_index("xy")
    guide = lax.axis_index("guide")
    col_y = lax.rem(xy, TILES_Y)
    col_x = xy // TILES_Y
    feet = [(0, 0), (0, 1)] + ([(1, 0), (1, 1)] if tiles_x > 1 else [])
    nf = len(feet)
    up_g = lax.rem(guide + 1, n_guide)
    down_g = lax.rem(guide + n_guide - 1, n_guide)
    slots = fluid_ref.shape[2]
    bands = levels // 8
    half = levels // 2
    load_f = pltpu.make_async_copy(f_hbm, o_ref, in_sem.at[0])
    load_c = pltpu.make_async_copy(c_hbm, c_ref, in_sem.at[1])
    load_m = pltpu.make_async_copy(m_hbm, m_ref, in_sem.at[2])
    load_f.start()

    @pl.when(grp == 0)
    def _():
        load_c.start()
        load_m.start()

    YU, YD, RIM, XA, XB = nf, nf + 1, nf + 2, nf + 6, nf + 7

    def foot_has(o, solid):
        dx, dy = feet[o]
        if solid:
            return jnp.logical_and(col_y + dy < TILES_Y, col_x + dx < tiles_x)
        return jnp.logical_and(col_y >= dy, col_x >= dx)

    def foot_xy(o, solid):
        dx, dy = feet[o]
        off = dx * TILES_Y + dy
        return lax.rem(xy + off, n_xy) if solid else lax.rem(xy + n_xy - off, n_xy)

    def copy(src, dst, ch, s, device):
        return pltpu.make_async_remote_copy(
            src_ref=src,
            dst_ref=dst,
            send_sem=send_sem.at[ch, s],
            recv_sem=recv_sem.at[ch, s],
            device_id=device,
            device_id_type=MESH,
        )

    def c_foot(o, s, solid):
        return copy(
            send_i.at[s, o],
            recv_i.at[s, o],
            o,
            s,
            {"grp": 1 - grp, "xy": foot_xy(o, solid)},
        )

    def c_up(s):
        return copy(send_y.at[0, s], recv_yu.at[s], YU, s, {"xy": lax.rem(xy + n_xy - 1, n_xy)})

    def c_down(s):
        return copy(send_y.at[1, s], recv_yd.at[s], YD, s, {"xy": lax.rem(xy + 1, n_xy)})

    def c_rim(kind, s, size):
        cols = pl.ds(0, size)
        return copy(
            send_rim.at[kind, s, :, cols],
            recv_rim.at[kind, s, :, cols],
            RIM + kind,
            s,
            {"guide": down_g if kind % 2 else up_g},
        )

    def c_x(which, s):
        off = n_xy - TILES_Y if which == 0 else TILES_Y
        return copy(
            send_x.at[which, s],
            recv_x.at[which, s],
            XA + which,
            s,
            {"xy": lax.rem(xy + off, n_xy)},
        )

    has_next_y = col_y < TILES_Y - 1
    has_prev_y = col_y > 0
    has_next_x = col_x < tiles_x - 1
    has_prev_x = col_x > 0

    barrier = pltpu.get_barrier_semaphore()

    def greet(device):
        pl.semaphore_signal(barrier, inc=1, device_id=device, device_id_type=MESH)

    greet({"guide": up_g})
    greet({"guide": down_g})
    for solid in (True, False):
        for o in range(nf):
            mine = (grp == 0) if solid else (grp != 0)

            @pl.when(jnp.logical_and(mine, foot_has(o, solid)))
            def _():
                greet({"grp": 1 - grp, "xy": foot_xy(o, solid)})

    sides = [(has_next_y, 1), (has_prev_y, n_xy - 1)]
    if tiles_x > 1:
        sides += [(has_next_x, TILES_Y), (has_prev_x, n_xy - TILES_Y)]
    for has, off in sides:

        @pl.when(jnp.logical_and(grp != 0, has))
        def _():
            greet({"xy": lax.rem(xy + off, n_xy)})

    def as_int(cond):
        return jnp.where(cond, 1, 0)

    solid_n = sum(as_int(foot_has(o, True)) for o in range(nf))
    fluid_n = sum(as_int(foot_has(o, False)) for o in range(nf)) + sum(as_int(h) for h, _ in sides)
    expect = 2 + jnp.where(grp == 0, solid_n, fluid_n)

    lane = iota((levels, LANES), 1)
    lane8 = iota((8, LANES), 1)
    level8 = iota((8, 1), 0)
    spot = iota((LANES, 1), 0)
    pick = iota((LANES, slots), 1) == iota((LANES, slots), 0) % slots
    diagonal = iota((LANES, LANES), 0) == iota((LANES, LANES), 1)

    def as_column(table):
        wide = jnp.concatenate(
            [jnp.broadcast_to(table[o : o + 1, :], (slots, slots)) for o in range(LANES // slots)],
            axis=0,
        )
        return jnp.sum(jnp.where(pick, wide.astype(F32), 0.0), axis=1, keepdims=True)

    def as_row(column):
        return jnp.sum(jnp.where(diagonal, column, 0.0), axis=0, keepdims=True)

    def slot_columns(table, owner_of):
        column = as_column(table)
        row = as_row(column).astype(jnp.int32)
        column = column.astype(jnp.int32)
        count = jnp.zeros((LANES, 1), jnp.int32)
        for o in range(nf):
            count = jnp.where(spot // slots == o, counts_ref[owner_of(o), o], count)
        return row, jnp.where(spot % slots < count, column, -1)

    def pack(samples, o):
        out = pltpu.roll(samples[0:8], (-o * slots) % LANES, 1)
        for b in range(1, bands):
            moved = pltpu.roll(samples[8 * b : 8 * b + 8], ((b - o) * slots) % LANES, 1)
            out = jnp.where(lane8 >= b * slots, moved, out)
        return out

    def unfold(packed):
        return jnp.concatenate([packed, pltpu.roll(packed, HALF, 1)], axis=0)

    left = iota((half, LANES), 1) < HALF

    def comp(ref, member, size, r0):
        return ref[r0 : r0 + 8, member * size : (member + 1) * size]

    def lower(member, size, r0, rim):
        if r0 == 0:
            block = comp(o_ref, member, size, 0)
            return jnp.where(level8 == 0, rim, pltpu.roll(block, 1, 0))
        return o_ref[r0 - 1 : r0 + 7, member * size : (member + 1) * size]

    def upper(member, size, r0, rim):
        if r0 == levels - 8:
            block = comp(o_ref, member, size, r0)
            return jnp.where(level8 == 7, rim, pltpu.roll(block, 7, 0))
        return o_ref[r0 + 1 : r0 + 9, member * size : (member + 1) * size]

    def gather(start, size, lanes):
        acc = None
        for c in range(0, size, CHUNK):
            part = dot(
                split3(o_ref[:, start + c : start + c + CHUNK]),
                g_ref[c : c + CHUNK, lanes[0] : lanes[1]],
            )
            acc = part if acc is None else acc + part
        return join3(acc)

    def incoming(s):
        blocks = []
        for b in range(bands):
            block = pltpu.roll(recv_i[s, 0], (-b * slots) % LANES, 1)
            for o in range(1, nf):
                moved = pltpu.roll(recv_i[s, o], ((o - b) * slots) % LANES, 1)
                block = jnp.where(lane8 >= o * slots, moved, block)
            blocks.append(block)
        return jnp.concatenate(blocks, axis=0)

    def each_foot(solid, act):
        for o in range(nf):

            @pl.when(foot_has(o, solid))
            def _():
                act(o)

    def send_feet(s, samples, solid):
        for o in reversed(range(nf)):
            send_i[s, o] = pack(samples, o)

            @pl.when(foot_has(o, solid))
            def _():
                c_foot(o, s, solid).start()

    def no_feet(solid):
        for o in range(1, nf):

            @pl.when(jnp.logical_not(foot_has(o, solid)))
            def _():
                recv_i[:, o] = jnp.zeros((STEPS, 8, LANES), F32)

    @pl.when(grp == 0)
    def _():
        no_feet(True)
        sides = sides_ref[0]
        row_idx, col_idx = slot_columns(sides // 2 * rc + rod_ref[0], lambda o: xy)
        face_col = 2.0 * as_column(sides % 2) - 1.0
        facing = as_row(face_col)
        for c in range(0, 2 * rc, CHUNK):
            g_ref[c : c + CHUNK, 0:LANES] = one_hot(iota((CHUNK, LANES), 0) + c == row_idx)
            at = iota((LANES, CHUNK), 1) + c == col_idx
            s_ref[0:LANES, c : c + CHUNK] = jnp.where(at, -face_col, 0.0).astype(BF16)
        mm_ref[0:LANES, 0:LANES] = jnp.where(
            col_idx == row_idx, -face_col * facing, 0.0
        ).astype(BF16)
        load_f.wait()

        def put_under(s):
            top = levels - 1
            send_rim[0, s, :, 0 : 2 * rc] = o_ref[top : top + 1, 7 * rc : 9 * rc]
            c_rim(0, s, 2 * rc).start()

        def put_over(s):
            send_rim[1, s, :, 0:rc] = o_ref[0:1, 5 * rc : 6 * rc]
            c_rim(1, s, rc).start()

        pl.semaphore_wait(barrier, expect)
        put_over(0)
        put_under(0)
        load_c.wait()
        load_m.wait()
        for r0 in range(0, levels, 8):
            soft = jnp.where(m_ref[r0 : r0 + 8, :] == 1, 1.0, SOFT_SHARE).astype(F32)
            lame_ref[r0 : r0 + 8, :] = c_ref[0, r0 : r0 + 8, :] * soft
            shear_ref[r0 : r0 + 8, :] = c_ref[1, r0 : r0 + 8, :] * soft
        acc = None
        for c in range(0, 2 * rc, CHUNK):
            part = dot(
                split3(c_ref[2, :, c % rc : c % rc + CHUNK]), g_ref[c : c + CHUNK, 0:LANES]
            )
            acc = part if acc is None else acc + part
        be_ref[...] = join3(acc)

        place = iota((1, rc), 1)
        in_x = place // S_ROD % S_ROD
        in_y = place % S_ROD

        def fore_x(v):
            return jnp.where(in_x < S_ROD - 1, pltpu.roll(v, rc - S_ROD, 1), 0.0) - v

        def back_x(v):
            return v - jnp.where(in_x > 0, pltpu.roll(v, S_ROD, 1), 0.0)

        def fore_y(v):
            return jnp.where(in_y < S_ROD - 1, pltpu.roll(v, rc - 1, 1), 0.0) - v

        def back_y(v):
            return v - jnp.where(in_y > 0, pltpu.roll(v, 1, 1), 0.0)

        def store(member, r0, v):
            o_ref[r0 : r0 + 8, member * rc : (member + 1) * rc] = v

        def step(s, carry):
            for r0 in [*range(8, levels, 8), 0]:
                if r0 == levels - 8:
                    c_rim(1, s, rc).wait_recv()
                if r0 == 0:
                    c_rim(0, s, 2 * rc).wait_recv()
                buo = c_ref[2, r0 : r0 + 8, :]
                xy_ = comp(o_ref, 6, rc, r0)
                xz = comp(o_ref, 7, rc, r0)
                yz = comp(o_ref, 8, rc, r0)
                xz_lo = lower(7, rc, r0, recv_rim[0, s, :, 0:rc])
                yz_lo = lower(8, rc, r0, recv_rim[0, s, :, rc : 2 * rc])
                store(
                    0,
                    r0,
                    comp(o_ref, 0, rc, r0)
                    + buo * (fore_x(comp(o_ref, 3, rc, r0)) + back_y(xy_) + (xz - xz_lo)),
                )
                store(
                    1,
                    r0,
                    comp(o_ref, 1, rc, r0)
                    + buo * (back_x(xy_) + fore_y(comp(o_ref, 4, rc, r0)) + (yz - yz_lo)),
                )
                zz = comp(o_ref, 5, rc, r0)
                zz_up = upper(5, rc, r0, recv_rim[1, s, :, 0:rc])
                store(
                    2,
                    r0,
                    comp(o_ref, 2, rc, r0) + buo * (back_x(xz) + back_y(yz) + (zz_up - zz)),
                )
                if r0 == levels - 8:
                    send_rim[2, s, :, 0:rc] = o_ref[levels - 1 : levels, 2 * rc : 3 * rc]
                    c_rim(2, s, rc).start()
            base = gather(0, 2 * rc, (0, LANES)) * facing
            each_foot(True, lambda o: c_foot(o, s, True).wait_recv())
            lhs = split3(incoming(s))
            normal = base + be_ref[...] * join3(dot(lhs, mm_ref[0:LANES, 0:LANES]))
            send_feet(s, normal, True)
            for c in range(0, 2 * rc, CHUNK):
                push = join3(dot(lhs, s_ref[0:LANES, c : c + CHUNK]))
                o_ref[:, c : c + CHUNK] += c_ref[2, :, c % rc : c % rc + CHUNK] * push
            send_rim[3, s, :, 0 : 2 * rc] = o_ref[0:1, 0 : 2 * rc]
            c_rim(3, s, 2 * rc).start()
            for r0 in [*range(8, levels - 8, 8), 0, levels - 8]:
                if r0 == 0:
                    c_rim(2, s, rc).wait_recv()
                if r0 == levels - 8:
                    c_rim(3, s, 2 * rc).wait_recv()
                sx = comp(o_ref, 0, rc, r0)
                sy = comp(o_ref, 1, rc, r0)
                sz = comp(o_ref, 2, rc, r0)
                lame = lame_ref[r0 : r0 + 8, :]
                shear = shear_ref[r0 : r0 + 8, :]
                spread_x = back_x(sx)
                spread_y = back_y(sy)
                spread_z = sz - lower(2, rc, r0, recv_rim[2, s, :, 0:rc])
                bulk = lame * (spread_x + spread_y + spread_z)
                twice = 2.0 * shear
                store(3, r0, comp(o_ref, 3, rc, r0) + bulk + twice * spread_x)
                store(4, r0, comp(o_ref, 4, rc, r0) + bulk + twice * spread_y)
                store(5, r0, comp(o_ref, 5, rc, r0) + bulk + twice * spread_z)
                store(6, r0, comp(o_ref, 6, rc, r0) + shear * (fore_y(sx) + fore_x(sy)))
                sx_up = upper(0, rc, r0, recv_rim[3, s, :, 0:rc])
                sy_up = upper(1, rc, r0, recv_rim[3, s, :, rc : 2 * rc])
                store(7, r0, comp(o_ref, 7, rc, r0) + shear * (sx_up - sx + fore_x(sz)))
                store(8, r0, comp(o_ref, 8, rc, r0) + shear * (sy_up - sy + fore_y(sz)))
                if r0 == 0:

                    @pl.when(s < STEPS - 1)
                    def _():
                        put_over(s + 1)

            @pl.when(s < STEPS - 1)
            def _():
                put_under(s + 1)

            return carry

        lax.fori_loop(0, STEPS, step, 0)

        def drain(s, carry):
            for kind, size in ((0, 2 * rc), (1, rc), (2, rc), (3, 2 * rc)):
                c_rim(kind, s, size).wait_send()
            each_foot(True, lambda o: c_foot(o, s, True).wait_send())
            return carry

        lax.fori_loop(0, STEPS, drain, 0)

    @pl.when(grp != 0)
    def _():
        no_feet(False)

        @pl.when(jnp.logical_not(has_next_y))
        def _():
            recv_yu[...] = jnp.zeros_like(recv_yu)

        @pl.when(jnp.logical_not(has_prev_y))
        def _():
            recv_yd[...] = jnp.zeros_like(recv_yd)

        if tiles_x > 1:

            @pl.when(jnp.logical_not(has_next_x))
            def _():
                recv_x[0] = jnp.zeros((STEPS, levels, LANES), F32)

            @pl.when(jnp.logical_not(has_prev_x))
            def _():
                recv_x[1] = jnp.zeros((STEPS, levels, LANES), F32)

        row_idx, col_idx = slot_columns(fluid_ref[0], lambda o: foot_xy(o, False))
        edge = iota((1, LANES), 1)
        edge_cols = jnp.where(
            edge < rows,
            edge * CY,
            jnp.where(
                jnp.logical_and(edge >= HALF, edge < HALF + rows),
                (edge - HALF) * CY + CY - 1,
                -2,
            ),
        )
        first_spots = jnp.where(spot < rows, spot * CY, -1)
        last_spots = jnp.where(spot < rows, spot * CY + CY - 1, -1)

        def put_rim(s):
            send_rim[1, s, :, 0:tc] = o_ref[0:1, 0:tc]
            c_rim(1, s, tc).start()
            if tiles_x > 1:
                send_x[0, s] = o_ref[:, 0:LANES]

                @pl.when(has_prev_x)
                def _():
                    c_x(0, s).start()

        def put_edges(s, edges):
            own_y[...] = edges
            send_y[0, s] = jnp.where(left, edges[:half], pltpu.roll(edges[half:], HALF, 1))
            send_y[1, s] = jnp.where(left, pltpu.roll(edges[:half], HALF, 1), edges[half:])

            @pl.when(has_prev_y)
            def _():
                c_up(s).start()

            @pl.when(has_next_y)
            def _():
                c_down(s).start()

        for c in range(0, tc, CHUNK):
            g_ref[c : c + CHUNK, 0:LANES] = one_hot(iota((CHUNK, LANES), 0) + c == row_idx)
            g_ref[c : c + CHUNK, LANES:] = one_hot(iota((CHUNK, LANES), 0) + c == edge_cols)
        load_f.wait()
        pl.semaphore_wait(barrier, expect)
        both = gather(0, tc, (0, 2 * LANES))
        send_feet(0, both[:, :LANES], False)
        put_edges(0, both[:, LANES:])
        put_rim(0)
        flows = gather(2 * tc, tc, (LANES, 2 * LANES))
        send_y[1, STEPS] = jnp.where(left, pltpu.roll(flows[:half], HALF, 1), flows[half:])

        @pl.when(has_next_y)
        def _():
            c_down(STEPS).start()

        for c in range(0, tc, CHUNK):
            at = iota((LANES, CHUNK), 1) + c
            s_ref[0:LANES, c : c + CHUNK] = one_hot(at == col_idx)
            s_ref[LANES:, c : c + CHUNK] = one_hot(at == first_spots)
            y_ref[:, c : c + CHUNK] = one_hot(at == last_spots)
        mm_ref[0:LANES, 0:LANES] = one_hot(col_idx == row_idx)
        mm_ref[0:LANES, LANES:] = one_hot(col_idx == edge_cols)
        mm_ref[LANES:, 0:LANES] = one_hot(first_spots == row_idx)
        mm_ref[LANES:, LANES:] = one_hot(first_spots == edge_cols)

        @pl.when(has_prev_y)
        def _():
            c_down(STEPS).wait_recv()

        be_ref[...] = jnp.where(lane < rows, unfold(recv_yd[STEPS]), 0.0)

        place = iota((1, tc), 1)
        in_y = place % CY

        def store(member, r0, v):
            o_ref[r0 : r0 + 8, member * tc : (member + 1) * tc] = v

        def step(s, carry):
            for r0 in range(0, levels, 8):
                if r0 == levels - 8:
                    c_rim(1, s, tc).wait_recv()
                p = comp(o_ref, 0, tc, r0)
                next_x = jnp.where(place < tc - CY, pltpu.roll(p, tc - CY, 1), 0.0)
                store(1, r0, comp(o_ref, 1, tc, r0) - FLUID_B * (next_x - p))
                next_y = jnp.where(in_y < CY - 1, pltpu.roll(p, tc - 1, 1), 0.0)
                store(2, r0, comp(o_ref, 2, tc, r0) - FLUID_B * (next_y - p))
                next_z = upper(0, tc, r0, recv_rim[1, s, :, 0:tc])
                store(3, r0, comp(o_ref, 3, tc, r0) - FLUID_B * (next_z - p))
            send_rim[2, s, :, 0:tc] = o_ref[levels - 1 : levels, 3 * tc : 4 * tc]
            c_rim(2, s, tc).start()
            if tiles_x > 1:

                @pl.when(has_next_x)
                def _():
                    c_x(0, s).wait_recv()

                ahead = pltpu.roll(recv_x[0, s], LANES - CY, 1)
                tail = slice(2 * tc - LANES, 2 * tc)
                o_ref[:, tail] -= jnp.where(lane >= LANES - CY, FLUID_B * ahead, 0.0)
                send_x[1, s] = o_ref[:, tail]

                @pl.when(has_next_x)
                def _():
                    c_x(1, s).start()

            @pl.when(has_next_y)
            def _():
                c_up(s).wait_recv()

            @pl.when(has_prev_y)
            def _():
                c_down(s).wait_recv()

            lhs = split3(unfold(recv_yu[s]))
            for c in range(0, tc, CHUNK):
                o_ref[:, 2 * tc + c : 2 * tc + c + CHUNK] -= FLUID_B * join3(
                    dot(lhs, y_ref[:, c : c + CHUNK])
                )
            behind = be_ref[...] - FLUID_B * (own_y[...] - unfold(recv_yd[s]))
            behind = jnp.where(jnp.logical_and(lane < rows, has_prev_y), behind, 0.0)
            be_ref[...] = behind

            for r0 in [*range(8, levels, 8), 0]:
                if r0 == 0:
                    c_rim(2, s, tc).wait_recv()
                fx = comp(o_ref, 1, tc, r0)
                fy = comp(o_ref, 2, tc, r0)
                fz = comp(o_ref, 3, tc, r0)
                prev_x = jnp.where(place >= CY, pltpu.roll(fx, CY, 1), 0.0)
                prev_y = jnp.where(in_y > 0, pltpu.roll(fy, 1, 1), 0.0)
                prev_z = lower(3, tc, r0, recv_rim[2, s, :, 0:tc])
                store(
                    0,
                    r0,
                    comp(o_ref, 0, tc, r0)
                    - FLUID_A * ((fx - prev_x) + (fy - prev_y) + (fz - prev_z)),
                )
            if tiles_x > 1:

                @pl.when(has_prev_x)
                def _():
                    c_x(1, s).wait_recv()

                before = pltpu.roll(recv_x[1, s], CY, 1)
                o_ref[:, 0:LANES] += jnp.where(lane < CY, FLUID_A * before, 0.0)

            @pl.when(s < STEPS - 1)
            def _():
                ebase_ref[...] = gather(0, tc, (0, 2 * LANES)) + FLUID_A * join3(
                    dot(split3(behind), mm_ref[LANES:, :])
                )

            each_foot(False, lambda o: c_foot(o, s, False).wait_recv())
            arrived = split3(incoming(s))

            @pl.when(s < STEPS - 1)
            def _():
                for part in (slice(0, LANES), slice(LANES, 2 * LANES)):
                    pushed = join3(dot(arrived, mm_ref[0:LANES, part]))
                    samples = ebase_ref[:, part] + FLUID_A * pushed
                    if part.start == 0:
                        send_feet(s + 1, samples, False)
                    else:
                        put_edges(s + 1, samples)

            lhs = jnp.concatenate([arrived, split3(behind)], axis=1)
            for c in range(0, tc, CHUNK):
                o_ref[:, c : c + CHUNK] += FLUID_A * join3(dot(lhs, s_ref[:, c : c + CHUNK]))

            @pl.when(s < STEPS - 1)
            def _():
                put_rim(s + 1)

            return carry

        lax.fori_loop(0, STEPS, step, 0)

        def drain(s, carry):
            c_rim(1, s, tc).wait_send()
            c_rim(2, s, tc).wait_send()
            each_foot(False, lambda o: c_foot(o, s, False).wait_send())

            @pl.when(has_prev_y)
            def _():
                c_up(s).wait_send()

            @pl.when(has_next_y)
            def _():
                c_down(s).wait_send()

            if tiles_x > 1:

                @pl.when(has_prev_x)
                def _():
                    c_x(0, s).wait_send()

                @pl.when(has_next_x)
                def _():
                    c_x(1, s).wait_send()

            return carry

        lax.fori_loop(0, STEPS, drain, 0)

        @pl.when(has_next_y)
        def _():
            c_down(STEPS).wait_send()


def local(n_xy, n_guide, fields, rod_coeffs, rod_mask, pair_counts, fluid_slots, rod_slots, rod_sides):
    levels, width = fields.shape[1:]
    rc, tc = width // 9, width // 4
    n_feet = 4 if n_xy > TILES_Y else 2
    n_x = 2 if n_xy > TILES_Y else 1
    x_steps = STEPS if n_xy > TILES_Y else 1
    rim = max(2 * rc, tc)
    vmem = pl.BlockSpec(memory_space=pltpu.VMEM)
    smem = pl.BlockSpec(memory_space=pltpu.SMEM)
    hbm = pl.BlockSpec(memory_space=pl.ANY)
    out = pl.pallas_call(
        functools.partial(kernel, n_xy, n_guide),
        out_shape=pltpu.VMEM((levels, width), F32),
        in_specs=[hbm, hbm, hbm, smem, vmem, vmem, vmem],
        out_specs=vmem,
        scratch_shapes=[
            pltpu.VMEM((3, levels, rc), F32),
            pltpu.VMEM((levels, rc), jnp.int32),
            pltpu.SemaphoreType.DMA((3,)),
            pltpu.VMEM((tc, 2 * LANES), BF16),
            pltpu.VMEM((2 * LANES, tc), BF16),
            pltpu.VMEM((LANES, tc), BF16),
            pltpu.VMEM((2 * LANES, 2 * LANES), BF16),
            pltpu.VMEM((levels, rc), F32),
            pltpu.VMEM((levels, rc), F32),
            pltpu.VMEM((levels, LANES), F32),
            pltpu.VMEM((levels, 2 * LANES), F32),
            pltpu.VMEM((STEPS, n_feet, 8, LANES), F32),
            pltpu.VMEM((STEPS, n_feet, 8, LANES), F32),
            pltpu.VMEM((levels, LANES), F32),
            pltpu.VMEM((2, STEPS + 1, levels // 2, LANES), F32),
            pltpu.VMEM((STEPS + 1, levels // 2, LANES), F32),
            pltpu.VMEM((STEPS + 1, levels // 2, LANES), F32),
            pltpu.VMEM((4, STEPS, 1, rim), F32),
            pltpu.VMEM((4, STEPS, 1, rim), F32),
            pltpu.VMEM((n_x, x_steps, levels, LANES), F32),
            pltpu.VMEM((n_x, x_steps, levels, LANES), F32),
            pltpu.SemaphoreType.DMA((n_feet + 8, STEPS + 1)),
            pltpu.SemaphoreType.DMA((n_feet + 8, STEPS + 1)),
        ],
        compiler_params=pltpu.CompilerParams(collective_id=0, has_side_effects=True),
    )(fields[0], rod_coeffs, rod_mask, pair_counts, fluid_slots, rod_slots, rod_sides)
    return out[None]


def solution(mesh):
    return jax.shard_map(
        functools.partial(local, mesh.shape["xy"], mesh.shape["guide"]),
        mesh=mesh,
        in_specs=(
            P("grp", "guide", "xy"),
            P(None, "guide", "xy"),
            P("guide", "xy"),
            P(),
            P("xy", None, None),
            P("xy", None, None),
            P("xy", None, None),
        ),
        out_specs=P("grp", "guide", "xy"),
        check_vma=False,
    )
```
